512 devices in a mesh: rows: 64 (over z, y), heads: 8 (over x, core).
Axes of the slice: x: 4, y: 8, z: 8, core: 2. Of those that a mesh axis runs over, the one named last changes fastest.
Arguments:
- queries: bfloat16 [8192, 8192], P('rows', 'heads'), may hold values from -128 to 128
- new_keys: bfloat16 [8192, 1024], P('rows', 'heads'), may hold values from -8 to 8
- new_values: bfloat16 [8192, 1024], P('rows', 'heads'), may hold values from -6 to 6
- library_keys: bfloat16 [1024, 128, 1024], P('rows', None, 'heads'), may hold values from -6 to 6
- library_values: bfloat16 [1024, 128, 1024], P('rows', None, 'heads'), may hold values from -6 to 6
- module_owner: int32 [64, 16], P('rows'), may hold values from 0 to 63, as said below
- module_page: int32 [64, 16], P('rows'), may hold values from 0 to 15
- module_count: int32 [64], P('rows'), may hold values from 1 to 16, 896 in all
Outputs:
- attended: bfloat16 [8192, 8192], P(('rows', 'heads'))
The draws below stay inside these ranges and needn't reach their ends.
Inputs may be any that keep to these rules, and one draw needn't show every extreme that they name: `module_owner`: among the 16 listed pages of the requests of one index of rows, live or not, no owner is named more than 2 times, and some owner exactly 2 times.
All inputs are finite; a program needn't handle non-finite values. No bound on the sum of `module_count` on one device may be relied on, other than what follows from the above.
Results may differ from the reference program's by a relative error of at most 0.0035.
Values may be sent and summed in bfloat16 or wider, within the bound.
A program may use at most 64 MiB of HBM per device.

```python
import math
import jax
import jax.numpy as jnp
import numpy as np
from jax import lax

HD = 128
QH = 64
KVH = 8
NEW_TOK = 128
PAGE = 128
MOD_MAX = 16
REQ_DEV = 1
PAGES_DEV = 16
REQUESTS = 64
TOKENS = 8192
PAGES = 1024
CAP = 2


def paired_fields(key):
    base = jax.random.fold_in(key, 17)
    first_key, second_key = jax.random.split(base, 2)
    group_size = QH // KVH
    query_field = jnp.clip(2.0 * jax.random.normal(first_key, (TOKENS, KVH, group_size, HD), jnp.float32), -12.0, 12.0)
    key_field = jnp.clip(jax.random.normal(second_key, (TOKENS, KVH, HD), jnp.float32), -6.0, 6.0)
    return (query_field.reshape(TOKENS, QH * HD), key_field.reshape(TOKENS, KVH * HD))


def draw_queries(key, part):
    return paired_fields(key)[0].astype(jnp.bfloat16)


def draw_new_keys(key, part):
    return paired_fields(key)[1].astype(jnp.bfloat16)


def draw_module_owner(key, part):
    base = jax.random.fold_in(key, 29)
    device_count = REQUESTS // REQ_DEV
    entries = REQ_DEV * MOD_MAX
    spot_count = device_count * CAP

    def one_device(device_key):
        perm_key, shuffle_key = jax.random.split(device_key)
        owners = (jax.random.permutation(perm_key, spot_count) // CAP).astype(jnp.int32)
        position = jnp.arange(spot_count, dtype=jnp.int32)
        ranked = jnp.where(owners == owners[0], position - spot_count, position)
        ordered = owners[jnp.argsort(ranked)]
        chosen = ordered[:entries]
        return chosen[jax.random.permutation(shuffle_key, entries)]
    device_keys = jax.random.split(base, device_count)
    return jax.vmap(one_device)(device_keys).reshape(REQUESTS, MOD_MAX).astype(jnp.int32)


def place_ends(values, own_key, least, high):
    index_at = [jax.random.randint(jax.random.fold_in(own_key, axis), (), 0, length) for axis, length in enumerate(values.shape)]
    longest = values.shape.index(max(values.shape))
    neighbour = index_at[:longest] + [(index_at[longest] + 1) % values.shape[longest]] + index_at[longest + 1:]
    return values.at[tuple(index_at)].set(least).at[tuple(neighbour)].set(high)


def levels(rng, dims, cuts, least, high):
    def one(dim, parts):
        draws = jax.random.uniform(jax.random.fold_in(jax.random.fold_in(rng, 6), dim), (parts,), jnp.float32, least / len(cuts), high / len(cuts))
        return jnp.repeat(jnp.exp(draws), dims[dim] // parts).reshape((-1,) + (1,) * (len(dims) - dim - 1))

    factor_of = one(*cuts[0])
    for cut in cuts[1:]:
        factor_of = factor_of * one(*cut)
    return factor_of


def split_up(count, total, limit, lean):
    portions = [(1 << 20) // math.isqrt(rank ** lean) + 1 for rank in range(2, count + 1)]
    rest, counts = total - limit - (count - 1), [1] * (count - 1)
    while rest > 0:
        candidates = [i for i in range(count - 1) if counts[i] < limit]
        whole, left = sum([portions[i] for i in candidates]), rest
        for i in candidates:
            extra = min(limit - counts[i], max(1, left * portions[i] // whole), rest)
            counts[i] = counts[i] + extra
            rest = rest - extra
    return np.array([limit] + counts)


def uneven(rng, number_of, total, most, skew):
    if number_of == 2:
        one = jax.random.randint(rng, (), max(1, total - most), min(most, total - 1) + 1)
        return jnp.stack([one, total - one])
    lengths = jnp.asarray(split_up(number_of, total, most, skew), jnp.int32)
    twos = (number_of - 1) // 2
    donor, sink = lengths[1:1 + 2 * twos:2], lengths[2:2 + 2 * twos:2]
    slack = jnp.minimum(donor - 1, most - sink)
    shifted = jax.random.randint(jax.random.fold_in(rng, 1), (twos,), 0, 1 << 20) % (slack + 1)
    lengths = lengths.at[1:1 + 2 * twos:2].set(donor - shifted).at[2:2 + 2 * twos:2].set(sink + shifted)
    return lengths[jax.random.permutation(jax.random.fold_in(rng, 2), number_of)]


def centred(own_key, extent, scale, most, cuts=(), held_as=jnp.bfloat16):
    drawn = jax.random.normal(own_key, extent, jnp.float32) * scale
    if len(cuts) > 0:
        drawn = levels(own_key, extent, cuts, -0.22, 0.18) * drawn
    return jnp.clip(drawn, min=-most, max=most).astype(held_as)


def setup_inputs(seed: int = 0) -> dict:
    key_of = jax.random.split(jax.random.key(seed), 9)
    return {
        "queries": draw_queries(jax.random.fold_in(key_of[8], 71), 0),
        "new_keys": draw_new_keys(jax.random.fold_in(key_of[8], 71), 0),
        "new_values": centred(key_of[2], (TOKENS, KVH * HD), 1.0, 6.0, ((0, 64), (1, 8))),
        "library_keys": centred(key_of[3], (PAGES, PAGE, KVH * HD), 1.0, 6.0, ((0, 64), (2, 8))),
        "library_values": centred(key_of[4], (PAGES, PAGE, KVH * HD), 1.0, 6.0, ((0, 64), (2, 8))),
        "module_owner": draw_module_owner(jax.random.fold_in(key_of[8], 71), 0),
        "module_page": place_ends(jax.random.randint(key_of[6], (REQUESTS, MOD_MAX), 0, PAGES_DEV), jax.random.fold_in(key_of[6], 1), 0, PAGES_DEV - 1).astype(jnp.int32),
        "module_count": uneven(key_of[7], REQUESTS, REQUESTS * MOD_MAX * 7 // 8, MOD_MAX, 2).astype(jnp.int32),
    }


def reference(queries, new_keys, new_values, library_keys, library_values, module_owner, module_page, module_count):
    group_size = QH // KVH
    score_scale = 1.0 / math.sqrt(HD)
    page_ids = (module_owner * PAGES_DEV + module_page).astype(jnp.int32)
    slot_live = jnp.arange(MOD_MAX, dtype=jnp.int32)[None, :] < module_count[:, None]
    library_live = jnp.repeat(slot_live, PAGE, axis=1)
    causal = jnp.arange(NEW_TOK)[None, :] <= jnp.arange(NEW_TOK)[:, None]
    query_all = queries.reshape(REQUESTS, NEW_TOK, KVH, group_size, HD)
    keys_new = new_keys.reshape(REQUESTS, NEW_TOK, KVH, HD)
    values_new = new_values.reshape(REQUESTS, NEW_TOK, KVH, HD)

    def one_request(request_item):
        query_rows, page_rows, live_rows, key_rows, value_rows = request_item
        library_k = library_keys[page_rows].reshape(MOD_MAX * PAGE, KVH, HD)
        library_v = library_values[page_rows].reshape(MOD_MAX * PAGE, KVH, HD)
        keys_all = jnp.concatenate([library_k, key_rows], axis=0).astype(jnp.float32)
        values_all = jnp.concatenate([library_v, value_rows], axis=0).astype(jnp.float32)
        scores = jnp.einsum('tkgd,skd->kgts', query_rows.astype(jnp.float32), keys_all) * score_scale
        allowed = jnp.concatenate([jnp.broadcast_to(live_rows[None, :], (NEW_TOK, MOD_MAX * PAGE)), causal], axis=1)
        scores = jnp.where(allowed, scores, -1e+30)
        row_max = lax.optimization_barrier(jnp.max(scores, axis=-1, keepdims=True))
        weights = jnp.where(allowed, jnp.exp(scores - row_max), 0.0)
        totals = lax.optimization_barrier(jnp.sum(weights, axis=-1))
        rounded = lax.optimization_barrier(weights.astype(jnp.bfloat16)).astype(jnp.float32)
        mixed_rows = jnp.einsum('kgts,skd->tkgd', rounded, values_all)
        mixed_rows = mixed_rows / jnp.transpose(totals, (2, 0, 1))[:, :, :, None]
        return mixed_rows.reshape(NEW_TOK, QH * HD).astype(jnp.bfloat16)
    result = lax.map(one_request, (query_all, page_ids, library_live, keys_new, values_new))
    return result.reshape(TOKENS, QH * HD)
```

```python
import functools
import math

import jax
import jax.numpy as jnp
from jax import lax
from jax.experimental import pallas as pl
from jax.experimental.pallas import tpu as pltpu
from jax.sharding import PartitionSpec as P

HD = 128
QH = 64
KVH = 8
GROUP = QH // KVH
MESH = pl.DeviceIdType.MESH
LOG2E = 1.4426950408889634
FLOOR = -1e30


def place(side):
    row = lax.axis_index("rows")
    core = lax.rem(lax.axis_index("heads"), 2)
    z, y = row // side, lax.rem(row, side)
    u = (1 - core) * z + core * y
    w = (1 - core) * y + core * z
    return core, u, w


def row_of(core, u, w, side):
    return (1 - core) * (u * side + w) + core * (w * side + u)


def wrap(value, side):
    return lax.rem(value + 4 * side, side)


def gather_kernel(side, k_in, v_in, q_in, t_in, k_all, v_all, q_all, t_all, send, recv, local):
    core, u, w = place(side)
    half = side // 2
    tokens = q_in.shape[0]
    lib_at = [row_of(core, wrap(u + d, side), w, side) for d in (1, -1)]
    que_at = [row_of(core, u, wrap(w + d, side), side) for d in (1, -1)]

    barrier = pltpu.get_barrier_semaphore()
    for row in lib_at + que_at:
        pl.semaphore_signal(barrier, inc=1, device_id={"rows": row}, device_id_type=MESH)
    pl.semaphore_wait(barrier, 4)

    own = [
        pltpu.make_async_copy(k_in, k_all.at[u], local.at[0]),
        pltpu.make_async_copy(v_in, v_all.at[u], local.at[1]),
        pltpu.make_async_copy(q_in, q_all.at[w], local.at[2]),
        pltpu.make_async_copy(t_in, t_all.at[w], local.at[3]),
    ]

    def parts(dirn, step):
        last = step == half - 1
        sign = (1, -1)[dirn]
        u0, w0 = wrap(u - sign * step, side), wrap(w - sign * step, side)
        lib, que = lib_at[dirn], que_at[dirn]
        first = step == 0
        rows = pl.ds((0, tokens // 2)[dirn], tokens // 2)
        k = ((k_in if first else k_all.at[u0]), k_all.at[u0], lib, 0)
        v = ((v_in if first else v_all.at[u0]), v_all.at[u0], lib, 1)
        t = ((t_in if first else t_all.at[w0]), t_all.at[w0], que, 3)
        if last:
            q = (q_all.at[w0, rows], q_all.at[w0, rows], que, 2)
            return [q, k, t] if dirn == 0 else [q, v]
        q = ((q_in if first else q_all.at[w0]), q_all.at[w0], que, 2)
        return [t, q, k, v] if dirn == 0 else [t, q, v, k]

    started = {}
    waited = set()

    def start(dirn, step, part):
        src, dst, row, kind = part
        copy = pltpu.make_async_remote_copy(
            src_ref=src,
            dst_ref=dst,
            send_sem=send.at[dirn, step, kind],
            recv_sem=recv.at[dirn, step, kind],
            device_id={"rows": row},
            device_id_type=MESH,
        )
        copy.start()
        started[dirn, step, kind] = copy

    for step in range(half):
        lists = [parts(dirn, step) for dirn in (0, 1)]
        for place_in_list in range(4):
            for dirn in (0, 1):
                if place_in_list >= len(lists[dirn]):
                    continue
                part = lists[dirn][place_in_list]
                before = (dirn, step - 1, part[3])
                if step > 0:
                    started[before].wait_recv()
                    waited.add(before)
                start(dirn, step, part)
        if step == 0:
            for copy in own:
                copy.start()
    for key, copy in started.items():
        if key not in waited:
            copy.wait_recv()
    for copy in started.values():
        copy.wait_send()
    for copy in own:
        copy.wait()


def gather_lines(k, v, q, t, side):
    half = side // 2
    shapes = [jax.ShapeDtypeStruct((side,) + a.shape, a.dtype) for a in (k, v, q, t)]
    anywhere = pl.BlockSpec(memory_space=pl.ANY)
    return pl.pallas_call(
        functools.partial(gather_kernel, side),
        out_shape=shapes,
        in_specs=[anywhere] * 4,
        out_specs=[anywhere] * 4,
        scratch_shapes=[
            pltpu.SemaphoreType.DMA((2, half, 4)),
            pltpu.SemaphoreType.DMA((2, half, 4)),
            pltpu.SemaphoreType.DMA((4,)),
        ],
        compiler_params=pltpu.CompilerParams(
            collective_id=0, has_side_effects=True, vmem_limit_bytes=48 << 20
        ),
        name="gather_lines",
    )(k, v, q, t)


def partial_kernel(
    side, codes, where_ref, q_ref, nk_ref, nv_ref, k_hbm, v_hbm, acc_out, stat_out, kbuf, vbuf, ksem, vsem, acc, stat
):
    step = pl.program_id(0)
    core, w = where_ref[0], where_ref[1]
    slots = kbuf.shape[0] // side
    pages = k_hbm.shape[1]
    scale = LOG2E / math.sqrt(HD)
    tokens = q_ref.shape[1]
    rows = GROUP * tokens

    def entry(req, slot):
        code = codes[req, 0, slot]
        owner, page = code // pages, lax.rem(code, pages)
        z, y = owner // side, lax.rem(owner, side)
        line = (1 - core) * z + core * y
        cross = (1 - core) * y + core * z
        mine = jnp.logical_and(code >= 0, cross == w)
        return mine, line, page

    def copies(req, slot, line, page):
        at = req * slots + slot
        return (
            pltpu.make_async_copy(k_hbm.at[line, page], kbuf.at[at], ksem.at[at]),
            pltpu.make_async_copy(v_hbm.at[line, page], vbuf.at[at], vsem.at[at]),
        )

    @pl.when(step == 0)
    def _():
        @pl.loop(0, side * slots)
        def _(at):
            req, slot = at // slots, lax.rem(at, slots)
            mine, line, page = entry(req, slot)

            @pl.when(mine)
            def _():
                for copy in copies(req, slot, line, page):
                    copy.start()

    wide = 2 * tokens

    def chunk_q(c):
        j = 2 * c
        return jnp.concatenate(
            [q_ref[0, :, j * HD : (j + 1) * HD], q_ref[0, :, (j + 1) * HD : (j + 2) * HD]], axis=0
        )

    def scores(keys, c):
        return lax.dot_general(
            keys, chunk_q(c), (((1,), (1,)), ((), ())), preferred_element_type=jnp.float32
        )

    def mix(values, weights):
        return lax.dot_general(
            values, weights.astype(jnp.bfloat16), (((0,), (0,)), ((), ())), preferred_element_type=jnp.float32
        )

    @pl.when(step != w)
    def _():
        acc[...] = jnp.zeros_like(acc)
        stat[0:1] = jnp.full((1, rows), FLOOR, jnp.float32)
        stat[1:2] = jnp.zeros((1, rows), jnp.float32)

    @pl.when(step == w)
    def _():
        keys, values = nk_ref[...], nv_ref[...]
        for c in range(rows // wide):
            cols = slice(c * wide, (c + 1) * wide)
            raw = scores(keys, c)
            key_at = lax.broadcasted_iota(jnp.int32, raw.shape, 0)
            token_at = lax.rem(lax.broadcasted_iota(jnp.int32, raw.shape, 1), tokens)
            allowed = key_at <= token_at
            raw = jnp.where(allowed, raw, FLOOR)
            top = jnp.max(raw, axis=0, keepdims=True) * scale
            weights = jnp.where(allowed, jnp.exp2(raw * scale - top), 0.0)
            stat[0:1, cols] = top
            stat[1:2, cols] = jnp.sum(weights, axis=0, keepdims=True)
            acc[:, cols] = mix(values, weights)

    @pl.loop(0, slots)
    def _(slot):
        mine, line, page = entry(step, slot)

        @pl.when(mine)
        def _():
            for copy in copies(step, slot, line, page):
                copy.wait()
            at = step * slots + slot
            keys, values = kbuf[at], vbuf[at]
            for c in range(rows // wide):
                cols = slice(c * wide, (c + 1) * wide)
                raw = scores(keys, c)
                old = stat[0:1, cols]
                top = jnp.maximum(old, jnp.max(raw, axis=0, keepdims=True) * scale)
                weights = jnp.exp2(raw * scale - top)
                shrink = jnp.exp2(old - top)
                stat[0:1, cols] = top
                stat[1:2, cols] = stat[1:2, cols] * shrink + jnp.sum(weights, axis=0, keepdims=True)
                acc[:, cols] = acc[:, cols] * shrink + mix(values, weights)

    acc_out[0] = acc[...]
    stat_out[0] = stat[...]


def partials(codes, where, q_all, nk, nv, k_all, v_all, side):
    tokens = q_all.shape[1]
    rows = GROUP * tokens
    slots = 16
    page = k_all.shape[2:]
    whole = lambda a: pl.BlockSpec(a.shape, lambda i: (0,) * a.ndim)
    return pl.pallas_call(
        functools.partial(partial_kernel, side),
        grid=(side,),
        out_shape=[
            jax.ShapeDtypeStruct((side, HD, rows), jnp.float32),
            jax.ShapeDtypeStruct((side, 2, rows), jnp.float32),
        ],
        in_specs=[
            pl.BlockSpec(memory_space=pltpu.SMEM),
            pl.BlockSpec(memory_space=pltpu.SMEM),
            pl.BlockSpec((1, tokens, GROUP * HD), lambda i: (i, 0, 0)),
            whole(nk),
            whole(nv),
            pl.BlockSpec(memory_space=pl.ANY),
            pl.BlockSpec(memory_space=pl.ANY),
        ],
        out_specs=[
            pl.BlockSpec((1, HD, rows), lambda i: (i, 0, 0)),
            pl.BlockSpec((1, 2, rows), lambda i: (i, 0, 0)),
        ],
        scratch_shapes=[
            pltpu.VMEM((side * slots,) + page, jnp.bfloat16),
            pltpu.VMEM((side * slots,) + page, jnp.bfloat16),
            pltpu.SemaphoreType.DMA((side * slots,)),
            pltpu.SemaphoreType.DMA((side * slots,)),
            pltpu.VMEM((HD, rows), jnp.float32),
            pltpu.VMEM((2, rows), jnp.float32),
        ],
        compiler_params=pltpu.CompilerParams(vmem_limit_bytes=48 << 20),
        name="partials",
    )(codes, where, q_all, nk, nv, k_all, v_all)


def return_kernel(
    side, acc_hbm, stat_hbm, out, accs, stats, acc_send, stat_send, acc_recv, stat_recv, result, send, recv, load, xsend, xrecv, xlocal
):
    core, u, w = place(side)
    me = lax.axis_index("heads")
    peers = lax.axis_size("heads")
    half = side // 2
    rows = accs.shape[2]
    part = rows // 2
    tokens = result.shape[0]
    share = tokens // peers
    near = [row_of(core, u, wrap(w + d, side), side) for d in (1, -1)]

    barrier = pltpu.get_barrier_semaphore()
    for row in near:
        pl.semaphore_signal(barrier, inc=1, device_id={"rows": row}, device_id_type=MESH)
    for hop in range(1, peers):
        pl.semaphore_signal(
            barrier, inc=1, device_id={"heads": lax.rem(me + hop, peers)}, device_id_type=MESH
        )
    order = [half, half - 1, half + 1] + [d for k in range(half - 2, 0, -1) for d in (k, side - k)] + [0]
    loads = {}
    for d in order:
        target = wrap(w + d, side)
        loads[d] = [
            pltpu.make_async_copy(acc_hbm.at[target], accs.at[target], load.at[d, 0]),
            pltpu.make_async_copy(stat_hbm.at[target], stats.at[target], load.at[d, 1]),
        ]
        for copy in loads[d]:
            copy.start()
    loaded = set()
    pl.semaphore_wait(barrier, 1 + peers)

    def cols(c):
        return slice(c * part, (c + 1) * part)

    def far(dirn, c):
        return half if dirn == c else half - 1

    flights = {}

    def launch(dirn, c, k, acc_src, stat_src):
        copies = [
            pltpu.make_async_remote_copy(
                src_ref=src,
                dst_ref=dst,
                send_sem=send.at[dirn, c, k, kind],
                recv_sem=recv.at[dirn, c, k, kind],
                device_id={"rows": near[dirn]},
                device_id_type=MESH,
            )
            for kind, (src, dst) in enumerate(
                [(stat_src, stat_recv.at[dirn, c, k]), (acc_src, acc_recv.at[dirn, c, k])]
            )
        ]
        for copy in copies:
            copy.start()
        flights[dirn, c, k] = copies

    def merge(one, two):
        (acc_a, stat_a), (acc_b, stat_b) = one, two
        top = jnp.maximum(stat_a[0:1], stat_b[0:1])
        fa, fb = jnp.exp2(stat_a[0:1] - top), jnp.exp2(stat_b[0:1] - top)
        total = stat_a[1:2] * fa + stat_b[1:2] * fb
        acc = acc_a.astype(jnp.float32) * fa + acc_b.astype(jnp.float32) * fb
        return acc, jnp.concatenate([top, total], axis=0)

    def arrived(dirn, c, k):
        for copy in flights[dirn, c, k]:
            copy.wait_recv()
        return acc_recv[dirn, c, k], stat_recv[dirn, c, k]

    def mine(d, c):
        if d % side not in loaded:
            loaded.add(d % side)
            for copy in loads[d % side]:
                copy.wait()
        target = wrap(w + d, side)
        return accs[target, :, cols(c)], stats[target, :, cols(c)]

    for k in range(half):
        for c in (0, 1):
            for dirn in (0, 1):
                reach = far(dirn, c) - k
                if reach < 1:
                    continue
                acc, stat = mine((1, -1)[dirn] * reach, c)
                if k > 0:
                    acc, stat = merge((acc, stat), arrived(dirn, c, k - 1))
                acc_send[dirn, c, k] = acc.astype(jnp.bfloat16)
                stat_send[dirn, c, k] = stat
                launch(dirn, c, k, acc_send.at[dirn, c, k], stat_send.at[dirn, c, k])

    exchange = []
    for c in (0, 1):
        total = mine(0, c)
        for dirn in (1, 0):
            total = merge(total, arrived(dirn, c, far(dirn, c) - 1))
        acc, stat = total
        final = acc / stat[1:2]
        for j in range(part // tokens):
            block = jnp.transpose(final[:, j * tokens : (j + 1) * tokens])
            at = c * part // tokens + j
            result[:, at * HD : (at + 1) * HD] = block.astype(result.dtype)
    width = result.shape[1]
    spot = pl.ds(pl.multiple_of(me * width, width), width)
    for hop in range(1, peers):
        peer = lax.rem(me + hop, peers)
        copy = pltpu.make_async_remote_copy(
            src_ref=result.at[pl.ds(pl.multiple_of(peer * share, share), share)],
            dst_ref=out.at[:, spot],
            send_sem=xsend.at[hop],
            recv_sem=xrecv.at[hop],
            device_id={"heads": peer},
            device_id_type=MESH,
        )
        copy.start()
        exchange.append(copy)
    keep = pltpu.make_async_copy(
        result.at[pl.ds(pl.multiple_of(me * share, share), share)], out.at[:, spot], xlocal
    )
    keep.start()
    for copy in exchange:
        copy.wait_recv()
    for copy in exchange:
        copy.wait_send()
    keep.wait()
    for copies in flights.values():
        for copy in copies:
            copy.wait_send()


def return_partials(acc_all, stat_all, side, peers):
    half = side // 2
    rows = acc_all.shape[2]
    tokens = rows // GROUP
    part = rows // 2
    width = GROUP * HD
    anywhere = pl.BlockSpec(memory_space=pl.ANY)
    return pl.pallas_call(
        functools.partial(return_kernel, side),
        out_shape=jax.ShapeDtypeStruct((tokens // peers, peers * width), jnp.bfloat16),
        in_specs=[anywhere] * 2,
        out_specs=anywhere,
        scratch_shapes=[
            pltpu.VMEM(acc_all.shape, jnp.float32),
            pltpu.VMEM(stat_all.shape, jnp.float32),
            pltpu.VMEM((2, 2, half, HD, part), jnp.bfloat16),
            pltpu.VMEM((2, 2, half, 2, part), jnp.float32),
            pltpu.VMEM((2, 2, half, HD, part), jnp.bfloat16),
            pltpu.VMEM((2, 2, half, 2, part), jnp.float32),
            pltpu.VMEM((tokens, width), jnp.bfloat16),
            pltpu.SemaphoreType.DMA((2, 2, half, 2)),
            pltpu.SemaphoreType.DMA((2, 2, half, 2)),
            pltpu.SemaphoreType.DMA((side, 2)),
            pltpu.SemaphoreType.DMA((peers,)),
            pltpu.SemaphoreType.DMA((peers,)),
            pltpu.SemaphoreType.DMA,
        ],
        compiler_params=pltpu.CompilerParams(
            collective_id=1, has_side_effects=True, vmem_limit_bytes=48 << 20
        ),
        name="return_partials",
    )(acc_all, stat_all)


def per_device(
    queries,
    new_keys,
    new_values,
    library_keys,
    library_values,
    module_owner,
    module_page,
    module_count,
):
    rows_count = lax.axis_size("rows")
    peers = lax.axis_size("heads")
    side = math.isqrt(rows_count)
    pages = library_keys.shape[0]
    slots = module_owner.shape[1]
    live = jnp.arange(slots, dtype=jnp.int32)[None, :] < module_count[:, None]
    codes = jnp.where(live, module_owner * pages + module_page, -1)
    codes = jnp.pad(codes, ((0, 0), (0, 128 - slots)), constant_values=-1)
    k_all, v_all, q_all, t_all = gather_lines(library_keys, library_values, queries, codes, side)
    core, _, w = place(side)
    where = jnp.stack([core, w]).astype(jnp.int32)
    acc_all, stat_all = partials(t_all, where, q_all, new_keys, new_values, k_all, v_all, side)
    return return_partials(acc_all, stat_all, side, peers)


def solution(mesh):
    placed = (
        P("rows", "heads"),
        P("rows", "heads"),
        P("rows", "heads"),
        P("rows", None, "heads"),
        P("rows", None, "heads"),
        P("rows", None),
        P("rows", None),
        P("rows"),
    )
    return jax.shard_map(
        per_device,
        mesh=mesh,
        in_specs=placed,
        out_specs=P(("rows", "heads"), None),
        check_vma=False,
    )
```

```python
import functools
import math

import jax
import jax.numpy as jnp
from jax import lax
from jax.experimental import pallas as pl
from jax.experimental.pallas import tpu as pltpu
from jax.sharding import PartitionSpec as P

HD = 128
QH = 64
KVH = 8
GROUP = QH // KVH
MESH = pl.DeviceIdType.MESH
LOG2E = 1.4426950408889634
FLOOR = -1e30


def place(side):
    row = lax.axis_index("rows")
    core = lax.rem(lax.axis_index("heads"), 2)
    z, y = row // side, lax.rem(row, side)
    u = (1 - core) * z + core * y
    w = (1 - core) * y + core * z
    return core, u, w


def row_of(core, u, w, side):
    return (1 - core) * (u * side + w) + core * (w * side + u)


def wrap(value, side):
    return lax.rem(value + 4 * side, side)


def gather_kernel(
    side, owner, page, count, k_in, v_in, q_in, k_all, v_all, q_all, t_all, vraw, qraw, vt, qt, table, send, recv, local
):
    core, u, w = place(side)
    half = side // 2
    heads_wide = qt.shape[1] // 2
    slots = owner.shape[1]
    pages = k_in.shape[0]
    tokens = qraw.shape[0]
    lib_at = [row_of(core, wrap(u + d, side), w, side) for d in (1, -1)]
    que_at = [row_of(core, u, wrap(w + d, side), side) for d in (1, -1)]

    barrier = pltpu.get_barrier_semaphore()
    for row in lib_at + que_at:
        pl.semaphore_signal(barrier, inc=1, device_id={"rows": row}, device_id_type=MESH)
    fetch_q = pltpu.make_async_copy(q_in, qraw, local.at[4])
    fetch_v = pltpu.make_async_copy(v_in, vraw, local.at[5])
    fetch_q.start()
    fetch_v.start()
    own = [pltpu.make_async_copy(k_in, k_all.at[u], local.at[0])]
    own[0].start()

    line_at = lax.broadcasted_iota(jnp.int32, table.shape, 0)
    lane_at = lax.broadcasted_iota(jnp.int32, table.shape, 1)
    filled = jnp.zeros(table.shape, jnp.int32)
    packed = jnp.zeros(table.shape, jnp.int32)
    for slot in range(slots):
        z, y = owner[0, slot] // side, lax.rem(owner[0, slot], side)
        line = (1 - core) * z + core * y
        cross = (1 - core) * y + core * z
        hit = jnp.logical_and(line_at == cross, count[0] > slot)
        packed = jnp.where(jnp.logical_and(hit, lane_at == filled), line * pages + page[0, slot], packed)
        filled = filled + jnp.where(hit, 1, 0)
    table[...] = jnp.where(lane_at == table.shape[1] - 1, filled, packed)

    started = {}
    waited = set()

    def start(dirn, step, kind):
        sign = (1, -1)[dirn]
        u0, w0 = wrap(u - sign * step, side), wrap(w - sign * step, side)
        if step > 0:
            started[dirn, step - 1, kind].wait_recv()
            waited.add((dirn, step - 1, kind))
        own_ref, all_ref, row = (
            (k_in, k_all.at[u0], lib_at[dirn]),
            (vt, v_all.at[u0], lib_at[dirn]),
            (qt, q_all.at[w0], que_at[dirn]),
            (table, t_all.at[w0], que_at[dirn]),
        )[kind]
        src, dst = (own_ref if step == 0 else all_ref), all_ref
        if kind == 2 and step == half - 1:
            cols = pl.ds(dirn * heads_wide, heads_wide)
            src, dst = all_ref.at[:, cols], all_ref.at[:, cols]
        copy = pltpu.make_async_remote_copy(
            src_ref=src,
            dst_ref=dst,
            send_sem=send.at[dirn, step, kind],
            recv_sem=recv.at[dirn, step, kind],
            device_id={"rows": row},
            device_id_type=MESH,
        )
        copy.start()
        started[dirn, step, kind] = copy

    def keep(src, dst, kind):
        copy = pltpu.make_async_copy(src, dst, local.at[kind])
        copy.start()
        own.append(copy)

    pl.semaphore_wait(barrier, 4)
    for dirn in (0, 1):
        start(dirn, 0, 3)
        start(dirn, 0, 0)
    fetch_q.wait()
    for j in range(GROUP):
        qt[:, j * tokens : (j + 1) * tokens] = jnp.transpose(qraw[:, j * HD : (j + 1) * HD])
    for dirn in (0, 1):
        start(dirn, 0, 2)
    fetch_v.wait()
    for j in range(pages):
        vt[j] = jnp.transpose(vraw[j])
    for dirn in (0, 1):
        start(dirn, 0, 1)
    keep(vt, v_all.at[u], 1)
    keep(qt, q_all.at[w], 2)
    keep(table, t_all.at[w], 3)
    for step in range(1, half):
        last = step == half - 1
        for kind in (3, 0, 2, 1):
            for dirn in (0, 1):
                if last and (dirn, kind) in ((1, 0), (0, 1), (1, 3)):
                    continue
                start(dirn, step, kind)
    for key, copy in started.items():
        if key not in waited:
            copy.wait_recv()
    for copy in started.values():
        copy.wait_send()
    for copy in own:
        copy.wait()


HBM = pl.BlockSpec(memory_space=pltpu.HBM)
SMEM = pl.BlockSpec(memory_space=pltpu.SMEM)
VMEM = pl.BlockSpec(memory_space=pltpu.VMEM)


def gather_lines(owner, page, count, k, v, q, side):
    half = side // 2
    tokens = q.shape[0]
    qt = (HD, GROUP * tokens)
    table = (side, 128)
    return pl.pallas_call(
        functools.partial(gather_kernel, side),
        out_shape=[
            jax.ShapeDtypeStruct((side,) + k.shape, k.dtype),
            jax.ShapeDtypeStruct((side,) + v.shape, v.dtype),
            jax.ShapeDtypeStruct((side,) + qt, q.dtype),
            jax.ShapeDtypeStruct((side,) + table, jnp.int32),
        ],
        in_specs=[SMEM] * 3 + [HBM] * 3,
        out_specs=[HBM] * 4,
        scratch_shapes=[
            pltpu.VMEM(v.shape, v.dtype),
            pltpu.VMEM(q.shape, q.dtype),
            pltpu.VMEM(v.shape, v.dtype),
            pltpu.VMEM(qt, q.dtype),
            pltpu.VMEM(table, jnp.int32),
            pltpu.SemaphoreType.DMA((2, half, 4)),
            pltpu.SemaphoreType.DMA((2, half, 4)),
            pltpu.SemaphoreType.DMA((6,)),
        ],
        compiler_params=pltpu.CompilerParams(
            collective_id=0, has_side_effects=True
        ),
        name="gather_lines",
    )(owner, page, count, k, v, q)


def partial_kernel(
    side, table, nk_ref, nv_ref, q_hbm, k_hbm, v_hbm, acc_out, stat_out, qbuf, kbuf, vbuf, acc, stat, qsem, ksem, vsem, osem
):
    _, _, w = place(side)
    slots = kbuf.shape[0] // side
    pages = k_hbm.shape[1]
    scale = LOG2E / math.sqrt(HD)
    rows = qbuf.shape[2]
    tokens = nk_ref.shape[0]
    wide = 2 * tokens
    chunks = [slice(c * wide, (c + 1) * wide) for c in range(rows // wide)]

    def listed(req):
        return table[req, w, table.shape[2] - 1]

    def page_copies(turn, k, value):
        at = turn * slots + k
        line, page = value // pages, lax.rem(value, pages)
        return (
            pltpu.make_async_copy(k_hbm.at[line, page], kbuf.at[at], ksem.at[at]),
            pltpu.make_async_copy(v_hbm.at[line, page], vbuf.at[at], vsem.at[at]),
        )

    def q_copy(turn):
        return pltpu.make_async_copy(q_hbm.at[wrap(w + turn, side)], qbuf.at[turn], qsem.at[turn])

    def out_copies(turn):
        spot, req = lax.rem(turn, 2), wrap(w + turn, side)
        return (
            pltpu.make_async_copy(acc.at[spot], acc_out.at[req], osem.at[spot, 0]),
            pltpu.make_async_copy(stat.at[spot], stat_out.at[req], osem.at[spot, 1]),
        )

    @pl.loop(0, side)
    def _(turn):
        q_copy(turn).start()
        req = wrap(w + turn, side)

        @pl.loop(0, listed(req))
        def _(k):
            for copy in page_copies(turn, k, table[req, w, k]):
                copy.start()

    def dot(one, two):
        return jnp.dot(one, two, preferred_element_type=jnp.float32)

    @pl.loop(0, side)
    def _(turn):
        spot, req = lax.rem(turn, 2), wrap(w + turn, side)

        @pl.when(turn >= 2)
        def _():
            for copy in out_copies(turn - 2):
                copy.wait()

        q_copy(turn).wait()

        @pl.when(turn > 0)
        def _():
            acc[spot] = jnp.zeros((HD, rows), jnp.float32)
            stat[spot, 0:1] = jnp.full((1, rows), FLOOR, jnp.float32)
            stat[spot, 1:2] = jnp.zeros((1, rows), jnp.float32)

        @pl.when(turn == 0)
        def _():
            keys, values = nk_ref[...], jnp.transpose(nv_ref[...])
            for cols in chunks:
                raw = dot(keys, qbuf[turn, :, cols])
                key_at = lax.broadcasted_iota(jnp.int32, raw.shape, 0)
                token_at = lax.rem(lax.broadcasted_iota(jnp.int32, raw.shape, 1), tokens)
                allowed = key_at <= token_at
                raw = jnp.where(allowed, raw, FLOOR)
                top = jnp.max(raw, axis=0, keepdims=True) * scale
                weights = jnp.where(allowed, jnp.exp2(raw * scale - top), 0.0)
                stat[spot, 0:1, cols] = top
                stat[spot, 1:2, cols] = jnp.sum(weights, axis=0, keepdims=True)
                acc[spot, :, cols] = dot(values, weights.astype(jnp.bfloat16))

        @pl.loop(0, listed(req))
        def _(k):
            for copy in page_copies(turn, k, table[req, w, k]):
                copy.wait()
            at = turn * slots + k
            keys, values = kbuf[at], vbuf[at]
            for cols in chunks:
                raw = dot(keys, qbuf[turn, :, cols])
                old = stat[spot, 0:1, cols]
                top = jnp.maximum(old, jnp.max(raw, axis=0, keepdims=True) * scale)
                weights = jnp.exp2(raw * scale - top)
                shrink = jnp.exp2(old - top)
                stat[spot, 0:1, cols] = top
                stat[spot, 1:2, cols] = stat[spot, 1:2, cols] * shrink + jnp.sum(weights, axis=0, keepdims=True)
                acc[spot, :, cols] = acc[spot, :, cols] * shrink + dot(values, weights.astype(jnp.bfloat16))

        for copy in out_copies(turn):
            copy.start()

    for turn in (side - 2, side - 1):
        for copy in out_copies(turn):
            copy.wait()


def partials(table, q_all, nk, nv, k_all, v_all, slots, side):
    rows = q_all.shape[2]
    page = k_all.shape[2:]
    return pl.pallas_call(
        functools.partial(partial_kernel, side),
        out_shape=[
            jax.ShapeDtypeStruct((side, HD, rows), jnp.float32),
            jax.ShapeDtypeStruct((side, 2, rows), jnp.float32),
        ],
        in_specs=[SMEM, VMEM, VMEM, HBM, HBM, HBM],
        out_specs=[HBM, HBM],
        scratch_shapes=[
            pltpu.VMEM(q_all.shape, jnp.bfloat16),
            pltpu.VMEM((side * slots,) + page, jnp.bfloat16),
            pltpu.VMEM((side * slots,) + page, jnp.bfloat16),
            pltpu.VMEM((2, HD, rows), jnp.float32),
            pltpu.VMEM((2, 2, rows), jnp.float32),
            pltpu.SemaphoreType.DMA((side,)),
            pltpu.SemaphoreType.DMA((side * slots,)),
            pltpu.SemaphoreType.DMA((side * slots,)),
            pltpu.SemaphoreType.DMA((2, 2)),
        ],
        name="partials",
    )(table, nk, nv, q_all, k_all, v_all)


def return_kernel(
    side, acc_hbm, stat_hbm, out, accs, stats, acc_send, stat_send, acc_recv, stat_recv, result, send, recv, load, xsend, xrecv, xlocal
):
    core, u, w = place(side)
    me = lax.axis_index("heads")
    peers = lax.axis_size("heads")
    half = side // 2
    rows = accs.shape[2]
    part = rows // 2
    tokens = result.shape[0]
    share = tokens // peers
    near = [row_of(core, u, wrap(w + d, side), side) for d in (1, -1)]

    barrier = pltpu.get_barrier_semaphore()
    for row in near:
        pl.semaphore_signal(barrier, inc=1, device_id={"rows": row}, device_id_type=MESH)
    for hop in range(1, peers):
        pl.semaphore_signal(
            barrier, inc=1, device_id={"heads": lax.rem(me + hop, peers)}, device_id_type=MESH
        )
    order = [half, half - 1, half + 1] + [d for k in range(half - 2, 0, -1) for d in (k, side - k)] + [0]
    loads = {}
    for d in order:
        target = wrap(w + d, side)
        loads[d] = [
            pltpu.make_async_copy(acc_hbm.at[target], accs.at[target], load.at[d, 0]),
            pltpu.make_async_copy(stat_hbm.at[target], stats.at[target], load.at[d, 1]),
        ]
        for copy in loads[d]:
            copy.start()
    loaded = set()
    pl.semaphore_wait(barrier, 1 + peers)

    def cols(c):
        return slice(c * part, (c + 1) * part)

    def far(dirn, c):
        return half if dirn == c else half - 1

    flights = {}

    def launch(dirn, c, k, acc_src, stat_src):
        copies = [
            pltpu.make_async_remote_copy(
                src_ref=src,
                dst_ref=dst,
                send_sem=send.at[dirn, c, k, kind],
                recv_sem=recv.at[dirn, c, k, kind],
                device_id={"rows": near[dirn]},
                device_id_type=MESH,
            )
            for kind, (src, dst) in enumerate(
                [(stat_src, stat_recv.at[dirn, c, k]), (acc_src, acc_recv.at[dirn, c, k])]
            )
        ]
        for copy in copies:
            copy.start()
        flights[dirn, c, k] = copies

    def merge(one, two):
        (acc_a, stat_a), (acc_b, stat_b) = one, two
        top = jnp.maximum(stat_a[0:1], stat_b[0:1])
        fa, fb = jnp.exp2(stat_a[0:1] - top), jnp.exp2(stat_b[0:1] - top)
        total = stat_a[1:2] * fa + stat_b[1:2] * fb
        acc = acc_a.astype(jnp.float32) * fa + acc_b.astype(jnp.float32) * fb
        return acc, jnp.concatenate([top, total], axis=0)

    def arrived(dirn, c, k):
        for copy in flights[dirn, c, k]:
            copy.wait_recv()
        return acc_recv[dirn, c, k], stat_recv[dirn, c, k]

    def mine(d, c):
        if d % side not in loaded:
            loaded.add(d % side)
            for copy in loads[d % side]:
                copy.wait()
        target = wrap(w + d, side)
        return accs[target, :, cols(c)], stats[target, :, cols(c)]

    for k in range(half):
        for c in (0, 1):
            for dirn in (0, 1):
                reach = far(dirn, c) - k
                if reach < 1:
                    continue
                acc, stat = mine((1, -1)[dirn] * reach, c)
                if k > 0:
                    acc, stat = merge((acc, stat), arrived(dirn, c, k - 1))
                acc_send[dirn, c, k] = acc.astype(jnp.bfloat16)
                stat_send[dirn, c, k] = stat
                launch(dirn, c, k, acc_send.at[dirn, c, k], stat_send.at[dirn, c, k])

    exchange = []
    for c in (0, 1):
        total = mine(0, c)
        for dirn in (1, 0):
            total = merge(total, arrived(dirn, c, far(dirn, c) - 1))
        acc, stat = total
        final = acc / stat[1:2]
        for j in range(part // tokens):
            block = jnp.transpose(final[:, j * tokens : (j + 1) * tokens])
            at = c * part // tokens + j
            result[:, at * HD : (at + 1) * HD] = block.astype(result.dtype)
    width = result.shape[1]
    spot = pl.ds(pl.multiple_of(me * width, width), width)
    for hop in range(1, peers):
        peer = lax.rem(me + hop, peers)
        copy = pltpu.make_async_remote_copy(
            src_ref=result.at[pl.ds(pl.multiple_of(peer * share, share), share)],
            dst_ref=out.at[:, spot],
            send_sem=xsend.at[hop],
            recv_sem=xrecv.at[hop],
            device_id={"heads": peer},
            device_id_type=MESH,
        )
        copy.start()
        exchange.append(copy)
    keep = pltpu.make_async_copy(
        result.at[pl.ds(pl.multiple_of(me * share, share), share)], out.at[:, spot], xlocal
    )
    keep.start()
    for copy in exchange:
        copy.wait_recv()
    for copy in exchange:
        copy.wait_send()
    keep.wait()
    for copies in flights.values():
        for copy in copies:
            copy.wait_send()


def return_partials(acc_all, stat_all, side, peers):
    half = side // 2
    rows = acc_all.shape[2]
    tokens = rows // GROUP
    part = rows // 2
    width = GROUP * HD
    return pl.pallas_call(
        functools.partial(return_kernel, side),
        out_shape=jax.ShapeDtypeStruct((tokens // peers, peers * width), jnp.bfloat16),
        in_specs=[HBM] * 2,
        out_specs=HBM,
        scratch_shapes=[
            pltpu.VMEM(acc_all.shape, jnp.float32),
            pltpu.VMEM(stat_all.shape, jnp.float32),
            pltpu.VMEM((2, 2, half, HD, part), jnp.bfloat16),
            pltpu.VMEM((2, 2, half, 2, part), jnp.float32),
            pltpu.VMEM((2, 2, half, HD, part), jnp.bfloat16),
            pltpu.VMEM((2, 2, half, 2, part), jnp.float32),
            pltpu.VMEM((tokens, width), jnp.bfloat16),
            pltpu.SemaphoreType.DMA((2, 2, half, 2)),
            pltpu.SemaphoreType.DMA((2, 2, half, 2)),
            pltpu.SemaphoreType.DMA((side, 2)),
            pltpu.SemaphoreType.DMA((peers,)),
            pltpu.SemaphoreType.DMA((peers,)),
            pltpu.SemaphoreType.DMA,
        ],
        compiler_params=pltpu.CompilerParams(
            collective_id=1, has_side_effects=True
        ),
        name="return_partials",
    )(acc_all, stat_all)


def per_device(
    queries,
    new_keys,
    new_values,
    library_keys,
    library_values,
    module_owner,
    module_page,
    module_count,
):
    rows_count = lax.axis_size("rows")
    peers = lax.axis_size("heads")
    side = math.isqrt(rows_count)
    slots = module_owner.shape[1]
    k_all, v_all, q_all, table = gather_lines(
        module_owner, module_page, module_count, library_keys, library_values, queries, side
    )
    acc_all, stat_all = partials(table, q_all, new_keys, new_values, k_all, v_all, slots, side)
    return return_partials(acc_all, stat_all, side, peers)


def solution(mesh):
    placed = (
        P("rows", "heads"),
        P("rows", "heads"),
        P("rows", "heads"),
        P("rows", None, "heads"),
        P("rows", None, "heads"),
        P("rows", None),
        P("rows", None),
        P("rows"),
    )
    return jax.shard_map(
        per_device,
        mesh=mesh,
        in_specs=placed,
        out_specs=P(("rows", "heads"), None),
        check_vma=False,
    )
```

```python
import functools
import math

import jax
import jax.numpy as jnp
from jax import lax
from jax.experimental import pallas as pl
from jax.experimental.pallas import tpu as pltpu
from jax.sharding import PartitionSpec as P

HD = 128
QH = 64
KVH = 8
GROUP = QH // KVH
MESH = pl.DeviceIdType.MESH
LOG2E = 1.4426950408889634
FLOOR = -1e30


def place(side):
    row = lax.axis_index("rows")
    core = lax.rem(lax.axis_index("heads"), 2)
    z, y = row // side, lax.rem(row, side)
    u = (1 - core) * z + core * y
    w = (1 - core) * y + core * z
    return core, u, w


def row_of(core, u, w, side):
    return (1 - core) * (u * side + w) + core * (w * side + u)


def wrap(value, side):
    return lax.rem(value + 4 * side, side)


def gather_kernel(
    side, owner_in, page_in, count, k_in, v_in, q_in, k_all, v_all, q_all, t_all, owner, page, vraw, qraw, send, recv, local
):
    core, u, w = place(side)
    half = side // 2
    heads_wide = q_all.shape[2] // 2
    shape = t_all.shape[1:]
    slots = owner.shape[1]
    pages = k_in.shape[0]
    tokens = qraw.shape[0]
    lib_at = [row_of(core, wrap(u + d, side), w, side) for d in (1, -1)]
    que_at = [row_of(core, u, wrap(w + d, side), side) for d in (1, -1)]

    barrier = pltpu.get_barrier_semaphore()
    for row in lib_at + que_at:
        pl.semaphore_signal(barrier, inc=1, device_id={"rows": row}, device_id_type=MESH)
    fetch_q = pltpu.make_async_copy(q_in, qraw, local.at[4])
    fetch_v = pltpu.make_async_copy(v_in, vraw, local.at[5])
    lists = [
        pltpu.make_async_copy(owner_in, owner, local.at[1]),
        pltpu.make_async_copy(page_in, page, local.at[2]),
    ]
    for copy in lists:
        copy.start()
    fetch_q.start()
    fetch_v.start()
    own = [pltpu.make_async_copy(k_in, k_all.at[u], local.at[0])]
    own[0].start()

    pl.semaphore_wait(barrier, 4)
    started = {}
    waited = set()

    def start(dirn, step, kind):
        sign = (1, -1)[dirn]
        u0, w0 = wrap(u - sign * step, side), wrap(w - sign * step, side)
        if step > 0:
            started[dirn, step - 1, kind].wait_recv()
            waited.add((dirn, step - 1, kind))
        all_ref, row = (
            (k_all.at[u0], lib_at[dirn]),
            (v_all.at[u0], lib_at[dirn]),
            (q_all.at[w0], que_at[dirn]),
            (t_all.at[w0], que_at[dirn]),
        )[kind]
        src, dst = (k_in if step == 0 and kind == 0 else all_ref), all_ref
        if kind == 2 and step == half - 1:
            cols = pl.ds(dirn * heads_wide, heads_wide)
            src, dst = all_ref.at[:, cols], all_ref.at[:, cols]
        copy = pltpu.make_async_remote_copy(
            src_ref=src,
            dst_ref=dst,
            send_sem=send.at[dirn, step, kind],
            recv_sem=recv.at[dirn, step, kind],
            device_id={"rows": row},
            device_id_type=MESH,
        )
        copy.start()
        started[dirn, step, kind] = copy

    for dirn in (0, 1):
        start(dirn, 0, 0)
    for copy in lists:
        copy.wait()
    line_at = lax.broadcasted_iota(jnp.int32, shape, 0)
    lane_at = lax.broadcasted_iota(jnp.int32, shape, 1)
    filled = jnp.zeros(shape, jnp.int32)
    packed = jnp.zeros(shape, jnp.int32)
    for slot in range(slots):
        z, y = owner[0, slot] // side, lax.rem(owner[0, slot], side)
        line = (1 - core) * z + core * y
        cross = (1 - core) * y + core * z
        hit = jnp.logical_and(line_at == cross, count[0] > slot)
        packed = jnp.where(jnp.logical_and(hit, lane_at == filled), line * pages + page[0, slot], packed)
        filled = filled + jnp.where(hit, 1, 0)
    t_all[w] = jnp.where(lane_at == shape[1] - 1, filled, packed)
    for dirn in (0, 1):
        start(dirn, 0, 3)
    fetch_q.wait()
    for j in range(GROUP):
        q_all[w, :, j * tokens : (j + 1) * tokens] = jnp.transpose(qraw[:, j * HD : (j + 1) * HD])
    for dirn in (0, 1):
        start(dirn, 0, 2)
    fetch_v.wait()
    for j in range(pages):
        v_all[u, j] = jnp.transpose(vraw[j])
    for dirn in (0, 1):
        start(dirn, 0, 1)
    for step in range(1, half):
        last = step == half - 1
        for kind in (3, 0, 2, 1):
            for dirn in (0, 1):
                if last and (dirn, kind) in ((1, 0), (0, 1), (1, 3)):
                    continue
                start(dirn, step, kind)
    for key, copy in started.items():
        if key not in waited:
            copy.wait_recv()
    for copy in started.values():
        copy.wait_send()
    for copy in own:
        copy.wait()


HBM = pl.BlockSpec(memory_space=pltpu.HBM)
SMEM = pl.BlockSpec(memory_space=pltpu.SMEM)
VMEM = pl.BlockSpec(memory_space=pltpu.VMEM)


def in_hbm(a):
    return pltpu.with_memory_space_constraint(a, pltpu.HBM)


def gather_lines(owner, page, count, k, v, q, side):
    half = side // 2
    tokens = q.shape[0]
    return pl.pallas_call(
        functools.partial(gather_kernel, side),
        out_shape=[
            pltpu.VMEM((side,) + k.shape, k.dtype),
            pltpu.VMEM((side,) + v.shape, v.dtype),
            pltpu.VMEM((side, HD, GROUP * tokens), q.dtype),
            pltpu.VMEM((side, side, 128), jnp.int32),
        ],
        in_specs=[HBM, HBM, SMEM, HBM, HBM, HBM],
        out_specs=[VMEM] * 4,
        scratch_shapes=[
            pltpu.SMEM(owner.shape, owner.dtype),
            pltpu.SMEM(page.shape, page.dtype),
            pltpu.VMEM(v.shape, v.dtype),
            pltpu.VMEM(q.shape, q.dtype),
            pltpu.SemaphoreType.DMA((2, half, 4)),
            pltpu.SemaphoreType.DMA((2, half, 4)),
            pltpu.SemaphoreType.DMA((6,)),
        ],
        compiler_params=pltpu.CompilerParams(
            collective_id=0, has_side_effects=True, vmem_limit_bytes=16 << 20
        ),
        name="gather_lines",
    )(in_hbm(owner), in_hbm(page), count, in_hbm(k), in_hbm(v), in_hbm(q))


def partial_kernel(side, table, nk_hbm, nv_hbm, q_all, k_all, v_all, acc, stat, nk, nv, fetched):
    _, _, w = place(side)
    pages = k_all.shape[1]
    scale = LOG2E / math.sqrt(HD)
    rows = q_all.shape[2]
    tokens = nk.shape[0]
    wide = 2 * tokens
    chunks = [slice(c * wide, (c + 1) * wide) for c in range(rows // wide)]
    fetches = [
        pltpu.make_async_copy(nk_hbm, nk, fetched.at[0]),
        pltpu.make_async_copy(nv_hbm, nv, fetched.at[1]),
    ]
    for copy in fetches:
        copy.start()

    def dot(one, two):
        return jnp.dot(one, two, preferred_element_type=jnp.float32)

    def add(req, keys, values, causal):
        for cols in chunks:
            raw = dot(keys, q_all[req, :, cols])
            if causal:
                key_at = lax.broadcasted_iota(jnp.int32, raw.shape, 0)
                token_at = lax.rem(lax.broadcasted_iota(jnp.int32, raw.shape, 1), tokens)
                allowed = key_at <= token_at
                raw = jnp.where(allowed, raw, FLOOR)
            old = stat[req, 0:1, cols]
            top = jnp.maximum(old, jnp.max(raw, axis=0, keepdims=True) * scale)
            weights = jnp.exp2(raw * scale - top)
            if causal:
                weights = jnp.where(allowed, weights, 0.0)
            shrink = jnp.exp2(old - top)
            stat[req, 0:1, cols] = top
            stat[req, 1:2, cols] = stat[req, 1:2, cols] * shrink + jnp.sum(weights, axis=0, keepdims=True)
            acc[req, :, cols] = acc[req, :, cols] * shrink + dot(values, weights.astype(jnp.bfloat16))

    @pl.loop(0, side)
    def _(req):
        acc[req] = jnp.zeros((HD, rows), jnp.float32)
        stat[req, 0:1] = jnp.full((1, rows), FLOOR, jnp.float32)
        stat[req, 1:2] = jnp.zeros((1, rows), jnp.float32)

        @pl.loop(0, table[req, w, table.shape[2] - 1])
        def _(k):
            value = table[req, w, k]
            line, page = value // pages, lax.rem(value, pages)
            add(req, k_all[line, page], v_all[line, page], False)

    for copy in fetches:
        copy.wait()
    add(w, nk[...], jnp.transpose(nv[...]), True)


def partials(table, q_all, nk, nv, k_all, v_all, side):
    rows = q_all.shape[2]
    return pl.pallas_call(
        functools.partial(partial_kernel, side),
        out_shape=[
            pltpu.VMEM((side, HD, rows), jnp.float32),
            pltpu.VMEM((side, 2, rows), jnp.float32),
        ],
        in_specs=[SMEM, HBM, HBM, VMEM, VMEM, VMEM],
        out_specs=[VMEM, VMEM],
        scratch_shapes=[
            pltpu.VMEM(nk.shape, nk.dtype),
            pltpu.VMEM(nv.shape, nv.dtype),
            pltpu.SemaphoreType.DMA((2,)),
        ],
        compiler_params=pltpu.CompilerParams(vmem_limit_bytes=16 << 20),
        name="partials",
    )(table, in_hbm(nk), in_hbm(nv), q_all, k_all, v_all)


def return_kernel(
    side, accs, stats, out, acc_send, stat_send, acc_recv, stat_recv, result, send, recv, xsend, xrecv, xlocal
):
    core, u, w = place(side)
    me = lax.axis_index("heads")
    peers = lax.axis_size("heads")
    half = side // 2
    rows = accs.shape[2]
    part = rows // 2
    tokens = result.shape[0]
    share = tokens // peers
    near = [row_of(core, u, wrap(w + d, side), side) for d in (1, -1)]

    barrier = pltpu.get_barrier_semaphore()
    for row in near:
        pl.semaphore_signal(barrier, inc=1, device_id={"rows": row}, device_id_type=MESH)
    for hop in range(1, peers):
        pl.semaphore_signal(
            barrier, inc=1, device_id={"heads": lax.rem(me + hop, peers)}, device_id_type=MESH
        )
    pl.semaphore_wait(barrier, 1 + peers)

    def cols(c):
        return slice(c * part, (c + 1) * part)

    def far(dirn, c):
        return half if dirn == c else half - 1

    flights = {}

    def launch(dirn, c, k, acc_src, stat_src):
        copies = [
            pltpu.make_async_remote_copy(
                src_ref=src,
                dst_ref=dst,
                send_sem=send.at[dirn, c, k, kind],
                recv_sem=recv.at[dirn, c, k, kind],
                device_id={"rows": near[dirn]},
                device_id_type=MESH,
            )
            for kind, (src, dst) in enumerate(
                [(stat_src, stat_recv.at[dirn, c, k]), (acc_src, acc_recv.at[dirn, c, k])]
            )
        ]
        for copy in copies:
            copy.start()
        flights[dirn, c, k] = copies

    def merge(one, two):
        (acc_a, stat_a), (acc_b, stat_b) = one, two
        top = jnp.maximum(stat_a[0:1], stat_b[0:1])
        fa, fb = jnp.exp2(stat_a[0:1] - top), jnp.exp2(stat_b[0:1] - top)
        total = stat_a[1:2] * fa + stat_b[1:2] * fb
        acc = acc_a.astype(jnp.float32) * fa + acc_b.astype(jnp.float32) * fb
        return acc, jnp.concatenate([top, total], axis=0)

    def arrived(dirn, c, k):
        for copy in flights[dirn, c, k]:
            copy.wait_recv()
        return acc_recv[dirn, c, k], stat_recv[dirn, c, k]

    def mine(d, c):
        target = wrap(w + d, side)
        return accs[target, :, cols(c)], stats[target, :, cols(c)]

    for k in range(half):
        for c in (0, 1):
            for dirn in (0, 1):
                reach = far(dirn, c) - k
                if reach < 1:
                    continue
                acc, stat = mine((1, -1)[dirn] * reach, c)
                if k > 0:
                    acc, stat = merge((acc, stat), arrived(dirn, c, k - 1))
                acc_send[dirn, c, k] = acc.astype(jnp.bfloat16)
                stat_send[dirn, c, k] = stat
                launch(dirn, c, k, acc_send.at[dirn, c, k], stat_send.at[dirn, c, k])

    exchange = []
    for c in (0, 1):
        total = mine(0, c)
        for dirn in (1, 0):
            total = merge(total, arrived(dirn, c, far(dirn, c) - 1))
        acc, stat = total
        final = acc / stat[1:2]
        for j in range(part // tokens):
            block = jnp.transpose(final[:, j * tokens : (j + 1) * tokens])
            at = c * part // tokens + j
            result[:, at * HD : (at + 1) * HD] = block.astype(result.dtype)
    width = result.shape[1]
    spot = pl.ds(pl.multiple_of(me * width, width), width)
    for hop in range(1, peers):
        peer = lax.rem(me + hop, peers)
        copy = pltpu.make_async_remote_copy(
            src_ref=result.at[pl.ds(pl.multiple_of(peer * share, share), share)],
            dst_ref=out.at[:, spot],
            send_sem=xsend.at[hop],
            recv_sem=xrecv.at[hop],
            device_id={"heads": peer},
            device_id_type=MESH,
        )
        copy.start()
        exchange.append(copy)
    keep = pltpu.make_async_copy(
        result.at[pl.ds(pl.multiple_of(me * share, share), share)], out.at[:, spot], xlocal
    )
    keep.start()
    for copy in exchange:
        copy.wait_recv()
    for copy in exchange:
        copy.wait_send()
    keep.wait()
    for copies in flights.values():
        for copy in copies:
            copy.wait_send()


def return_partials(acc_all, stat_all, side, peers):
    half = side // 2
    rows = acc_all.shape[2]
    tokens = rows // GROUP
    part = rows // 2
    width = GROUP * HD
    return pl.pallas_call(
        functools.partial(return_kernel, side),
        out_shape=jax.ShapeDtypeStruct((tokens // peers, peers * width), jnp.bfloat16),
        in_specs=[VMEM] * 2,
        out_specs=HBM,
        scratch_shapes=[
            pltpu.VMEM((2, 2, half, HD, part), jnp.bfloat16),
            pltpu.VMEM((2, 2, half, 2, part), jnp.float32),
            pltpu.VMEM((2, 2, half, HD, part), jnp.bfloat16),
            pltpu.VMEM((2, 2, half, 2, part), jnp.float32),
            pltpu.VMEM((tokens, width), jnp.bfloat16),
            pltpu.SemaphoreType.DMA((2, 2, half, 2)),
            pltpu.SemaphoreType.DMA((2, 2, half, 2)),
            pltpu.SemaphoreType.DMA((peers,)),
            pltpu.SemaphoreType.DMA((peers,)),
            pltpu.SemaphoreType.DMA,
        ],
        compiler_params=pltpu.CompilerParams(
            collective_id=1, has_side_effects=True, vmem_limit_bytes=16 << 20
        ),
        name="return_partials",
    )(acc_all, stat_all)


def per_device(
    queries,
    new_keys,
    new_values,
    library_keys,
    library_values,
    module_owner,
    module_page,
    module_count,
):
    rows_count = lax.axis_size("rows")
    peers = lax.axis_size("heads")
    side = math.isqrt(rows_count)
    k_all, v_all, q_all, table = gather_lines(
        module_owner, module_page, module_count, library_keys, library_values, queries, side
    )
    acc_all, stat_all = partials(table, q_all, new_keys, new_values, k_all, v_all, side)
    return return_partials(acc_all, stat_all, side, peers)


def solution(mesh):
    placed = (
        P("rows", "heads"),
        P("rows", "heads"),
        P("rows", "heads"),
        P("rows", None, "heads"),
        P("rows", None, "heads"),
        P("rows", None),
        P("rows", None),
        P("rows"),
    )
    return jax.shard_map(
        per_device,
        mesh=mesh,
        in_specs=placed,
        out_specs=P(("rows", "heads"), None),
        check_vma=False,
    )
```

```python
import functools
import math

import jax
import jax.numpy as jnp
from jax import lax
from jax.experimental import pallas as pl
from jax.experimental.pallas import tpu as pltpu
from jax.sharding import PartitionSpec as P

HD = 128
QH = 64
KVH = 8
GROUP = QH // KVH
MESH = pl.DeviceIdType.MESH
LOG2E = 1.4426950408889634
FLOOR = -1e30


def place(side):
    row = lax.axis_index("rows")
    core = lax.rem(lax.axis_index("heads"), 2)
    z, y = row // side, lax.rem(row, side)
    u = (1 - core) * z + core * y
    w = (1 - core) * y + core * z
    return core, u, w


def row_of(core, u, w, side):
    return (1 - core) * (u * side + w) + core * (w * side + u)


def wrap(value, side):
    return lax.rem(value + 4 * side, side)


def gather_kernel(
    side, owner_in, page_in, count, k_in, v_in, q_in, k_all, v_all, q_all, t_all, owner, page, vraw, qraw, send, recv, local
):
    core, u, w = place(side)
    half = side // 2
    heads_wide = q_all.shape[2] // 2
    shape = t_all.shape[1:]
    slots = owner.shape[1]
    pages = k_in.shape[0]
    tokens = qraw.shape[0]
    lib_at = [row_of(core, wrap(u + d, side), w, side) for d in (1, -1)]
    que_at = [row_of(core, u, wrap(w + d, side), side) for d in (1, -1)]

    barrier = pltpu.get_barrier_semaphore()
    for row in lib_at + que_at:
        pl.semaphore_signal(barrier, inc=1, device_id={"rows": row}, device_id_type=MESH)
    fetch_q = pltpu.make_async_copy(q_in, qraw, local.at[4])
    fetch_v = pltpu.make_async_copy(v_in, vraw, local.at[5])
    lists = [
        pltpu.make_async_copy(owner_in, owner, local.at[1]),
        pltpu.make_async_copy(page_in, page, local.at[2]),
    ]
    for copy in lists:
        copy.start()
    fetch_q.start()
    fetch_v.start()
    own = [pltpu.make_async_copy(k_in, k_all.at[u], local.at[0])]
    own[0].start()

    pl.semaphore_wait(barrier, 4)
    started = {}
    waited = set()

    def start(dirn, step, kind):
        sign = (1, -1)[dirn]
        u0, w0 = wrap(u - sign * step, side), wrap(w - sign * step, side)
        if step > 0:
            started[dirn, step - 1, kind].wait_recv()
            waited.add((dirn, step - 1, kind))
        all_ref, row = (
            (k_all.at[u0], lib_at[dirn]),
            (v_all.at[u0], lib_at[dirn]),
            (q_all.at[w0], que_at[dirn]),
            (t_all.at[w0], que_at[dirn]),
        )[kind]
        src, dst = (k_in if step == 0 and kind == 0 else all_ref), all_ref
        if kind == 2 and step == half - 1:
            cols = pl.ds(dirn * heads_wide, heads_wide)
            src, dst = all_ref.at[:, cols], all_ref.at[:, cols]
        copy = pltpu.make_async_remote_copy(
            src_ref=src,
            dst_ref=dst,
            send_sem=send.at[dirn, step, kind],
            recv_sem=recv.at[dirn, step, kind],
            device_id={"rows": row},
            device_id_type=MESH,
        )
        copy.start()
        started[dirn, step, kind] = copy

    for dirn in (0, 1):
        start(dirn, 0, 0)
    for copy in lists:
        copy.wait()
    line_at = lax.broadcasted_iota(jnp.int32, shape, 0)
    lane_at = lax.broadcasted_iota(jnp.int32, shape, 1)
    filled = jnp.zeros(shape, jnp.int32)
    packed = jnp.zeros(shape, jnp.int32)
    for slot in range(slots):
        z, y = owner[0, slot] // side, lax.rem(owner[0, slot], side)
        line = (1 - core) * z + core * y
        cross = (1 - core) * y + core * z
        hit = jnp.logical_and(line_at == cross, count[0] > slot)
        packed = jnp.where(jnp.logical_and(hit, lane_at == filled), line * pages + page[0, slot], packed)
        filled = filled + jnp.where(hit, 1, 0)
    t_all[w] = jnp.where(lane_at == shape[1] - 1, filled, packed)
    for dirn in (0, 1):
        start(dirn, 0, 3)
    fetch_q.wait()
    for j in range(GROUP):
        q_all[w, :, j * tokens : (j + 1) * tokens] = jnp.transpose(qraw[:, j * HD : (j + 1) * HD])
    for dirn in (0, 1):
        start(dirn, 0, 2)
    fetch_v.wait()
    for j in range(pages):
        v_all[u, j] = jnp.transpose(vraw[j])
    for dirn in (0, 1):
        start(dirn, 0, 1)
    for step in range(1, half):
        last = step == half - 1
        for kind in (3, 0, 2, 1):
            for dirn in (0, 1):
                if last and (dirn, kind) in ((1, 0), (0, 1), (1, 3)):
                    continue
                start(dirn, step, kind)
    for key, copy in started.items():
        if key not in waited:
            copy.wait_recv()
    for copy in started.values():
        copy.wait_send()
    for copy in own:
        copy.wait()


HBM = pl.BlockSpec(memory_space=pltpu.HBM)
SMEM = pl.BlockSpec(memory_space=pltpu.SMEM)
VMEM = pl.BlockSpec(memory_space=pltpu.VMEM)


def in_hbm(a):
    return pltpu.with_memory_space_constraint(a, pltpu.HBM)


def gather_lines(owner, page, count, k, v, q, side):
    half = side // 2
    tokens = q.shape[0]
    return pl.pallas_call(
        functools.partial(gather_kernel, side),
        out_shape=[
            pltpu.VMEM((side,) + k.shape, k.dtype),
            pltpu.VMEM((side,) + v.shape, v.dtype),
            pltpu.VMEM((side, HD, GROUP * tokens), q.dtype),
            pltpu.VMEM((side, side, 128), jnp.int32),
        ],
        in_specs=[HBM, HBM, SMEM, HBM, HBM, HBM],
        out_specs=[VMEM] * 4,
        scratch_shapes=[
            pltpu.SMEM(owner.shape, owner.dtype),
            pltpu.SMEM(page.shape, page.dtype),
            pltpu.VMEM(v.shape, v.dtype),
            pltpu.VMEM(q.shape, q.dtype),
            pltpu.SemaphoreType.DMA((2, half, 4)),
            pltpu.SemaphoreType.DMA((2, half, 4)),
            pltpu.SemaphoreType.DMA((6,)),
        ],
        compiler_params=pltpu.CompilerParams(
            collective_id=0, has_side_effects=True, vmem_limit_bytes=16 << 20
        ),
        name="gather_lines",
    )(in_hbm(owner), in_hbm(page), count, in_hbm(k), in_hbm(v), in_hbm(q))


def partial_kernel(side, table, nk_hbm, nv_hbm, q_all, k_all, v_all, acc, stat, nk, nv, fetched):
    _, _, w = place(side)
    pages = k_all.shape[1]
    scale = LOG2E / math.sqrt(HD)
    rows = q_all.shape[2]
    tokens = nk.shape[0]
    wide = 2 * tokens
    chunks = [slice(c * wide, (c + 1) * wide) for c in range(rows // wide)]
    fetches = [
        pltpu.make_async_copy(nk_hbm, nk, fetched.at[0]),
        pltpu.make_async_copy(nv_hbm, nv, fetched.at[1]),
    ]
    for copy in fetches:
        copy.start()

    def dot(one, two):
        return jnp.dot(one, two, preferred_element_type=jnp.float32)

    def add(req, keys, values, causal):
        for cols in chunks:
            raw = dot(keys, q_all[req, :, cols])
            if causal:
                key_at = lax.broadcasted_iota(jnp.int32, raw.shape, 0)
                token_at = lax.rem(lax.broadcasted_iota(jnp.int32, raw.shape, 1), tokens)
                allowed = key_at <= token_at
                raw = jnp.where(allowed, raw, FLOOR)
            old = stat[req, 0:1, cols]
            top = jnp.maximum(old, jnp.max(raw, axis=0, keepdims=True) * scale)
            weights = jnp.exp2(raw * scale - top)
            if causal:
                weights = jnp.where(allowed, weights, 0.0)
            shrink = jnp.exp2(old - top)
            stat[req, 0:1, cols] = top
            stat[req, 1:2, cols] = stat[req, 1:2, cols] * shrink + jnp.sum(weights, axis=0, keepdims=True)
            acc[req, :, cols] = acc[req, :, cols] * shrink + dot(values, weights.astype(jnp.bfloat16))

    @pl.loop(0, side)
    def _(req):
        acc[req] = jnp.zeros((HD, rows), jnp.float32)
        stat[req, 0:1] = jnp.full((1, rows), FLOOR, jnp.float32)
        stat[req, 1:2] = jnp.zeros((1, rows), jnp.float32)

        @pl.loop(0, table[req, w, table.shape[2] - 1])
        def _(k):
            value = table[req, w, k]
            line, page = value // pages, lax.rem(value, pages)
            add(req, k_all[line, page], v_all[line, page], False)

    for copy in fetches:
        copy.wait()
    add(w, nk[...], jnp.transpose(nv[...]), True)


def partials(table, q_all, nk, nv, k_all, v_all, side):
    rows = q_all.shape[2]
    return pl.pallas_call(
        functools.partial(partial_kernel, side),
        out_shape=[
            pltpu.VMEM((side, HD, rows), jnp.float32),
            pltpu.VMEM((side, 2, rows), jnp.float32),
        ],
        in_specs=[SMEM, HBM, HBM, VMEM, VMEM, VMEM],
        out_specs=[VMEM, VMEM],
        scratch_shapes=[
            pltpu.VMEM(nk.shape, nk.dtype),
            pltpu.VMEM(nv.shape, nv.dtype),
            pltpu.SemaphoreType.DMA((2,)),
        ],
        compiler_params=pltpu.CompilerParams(vmem_limit_bytes=16 << 20),
        name="partials",
    )(table, in_hbm(nk), in_hbm(nv), q_all, k_all, v_all)


def return_kernel(side, accs, stats, out, outgoing, incoming, result, send, recv, xsend, xrecv, xlocal):
    core, u, w = place(side)
    me = lax.axis_index("heads")
    peers = lax.axis_size("heads")
    half = side // 2
    chunks = outgoing.shape[1]
    part = outgoing.shape[4]
    extra = outgoing.shape[3] - HD
    tokens, width = result.shape
    share = tokens // peers
    near = [row_of(core, u, wrap(w + d, side), side) for d in (1, -1)]

    barrier = pltpu.get_barrier_semaphore()
    for row in near:
        pl.semaphore_signal(barrier, inc=1, device_id={"rows": row}, device_id_type=MESH)
    for hop in range(1, peers):
        pl.semaphore_signal(
            barrier, inc=1, device_id={"heads": lax.rem(me + hop, peers)}, device_id_type=MESH
        )

    def far(dirn, c):
        return half if c % 2 == dirn else half - 1

    def mine(d, c):
        target, cols = wrap(w + d, side), slice(c * part, (c + 1) * part)
        return accs[target, :, cols], stats[target, 0:1, cols], stats[target, 1:2, cols]

    def split(value):
        pieces = []
        for _ in range(3):
            pieces.append(value.astype(jnp.bfloat16).astype(jnp.float32))
            value = value - pieces[-1]
        return pieces

    row_at = lax.broadcasted_iota(jnp.int32, (extra, part), 0)

    def pack(ref, item):
        acc, top, total = item
        ref[0:HD] = acc.astype(jnp.bfloat16)
        tail = jnp.zeros((extra, part), jnp.float32)
        for i, piece in enumerate(split(top) + split(total)):
            tail = jnp.where(row_at == i, piece, tail)
        ref[HD : HD + extra] = tail.astype(jnp.bfloat16)

    def unpack(ref):
        tail = ref[HD : HD + extra].astype(jnp.float32)
        top = tail[0:1] + tail[1:2] + tail[2:3]
        total = tail[3:4] + tail[4:5] + tail[5:6]
        return ref[0:HD].astype(jnp.float32), top, total

    def merge(one, two):
        top = jnp.maximum(one[1], two[1])
        fa, fb = jnp.exp2(one[1] - top), jnp.exp2(two[1] - top)
        return one[0] * fa + two[0] * fb, top, one[2] * fa + two[2] * fb

    flights = {}

    def launch(dirn, c, k):
        copy = pltpu.make_async_remote_copy(
            src_ref=outgoing.at[dirn, c, k],
            dst_ref=incoming.at[dirn, c, k],
            send_sem=send.at[dirn, c, k],
            recv_sem=recv.at[dirn, c, k],
            device_id={"rows": near[dirn]},
            device_id_type=MESH,
        )
        copy.start()
        flights[dirn, c, k] = copy

    def arrived(dirn, c, k):
        flights[dirn, c, k].wait_recv()
        return unpack(incoming.at[dirn, c, k])

    starts = [(c, dirn) for c in range(chunks) for dirn in (0, 1)]
    for c, dirn in starts:
        pack(outgoing.at[dirn, c, 0], mine((1, -1)[dirn] * far(dirn, c), c))
    pl.semaphore_wait(barrier, 1 + peers)
    for c, dirn in starts:
        launch(dirn, c, 0)
    for k in range(1, half):
        for c, dirn in starts:
            reach = far(dirn, c) - k
            if reach < 1:
                continue
            item = mine((1, -1)[dirn] * reach, c)
            pack(outgoing.at[dirn, c, k], merge(item, arrived(dirn, c, k - 1)))
            launch(dirn, c, k)

    exchange = []
    groups = exchange_groups(chunks)
    for g, group in enumerate(groups):
        for c in group:
            item = mine(0, c)
            for dirn in sorted((0, 1), key=lambda dirn: far(dirn, c)):
                item = merge(item, arrived(dirn, c, far(dirn, c) - 1))
            final = item[0] / item[2]
            for j in range(part // tokens):
                at = c * part // tokens + j
                block = jnp.transpose(final[:, j * tokens : (j + 1) * tokens])
                result[:, at * HD : (at + 1) * HD] = block.astype(result.dtype)
        first, size = group[0] * part, len(group) * part
        here = slice(first, first + size)
        there = pl.ds(pl.multiple_of(me * width + first, size), size)
        for hop in range(1, peers):
            peer = lax.rem(me + hop, peers)
            copy = pltpu.make_async_remote_copy(
                src_ref=result.at[pl.ds(pl.multiple_of(peer * share, share), share), here],
                dst_ref=out.at[:, there],
                send_sem=xsend.at[g, hop],
                recv_sem=xrecv.at[g, hop],
                device_id={"heads": peer},
                device_id_type=MESH,
            )
            copy.start()
            exchange.append(copy)
        keep = pltpu.make_async_copy(
            result.at[pl.ds(pl.multiple_of(me * share, share), share), here], out.at[:, there], xlocal.at[g]
        )
        keep.start()
        exchange.append(keep)
    for copy in exchange:
        copy.wait()
    for copy in flights.values():
        copy.wait_send()


def exchange_groups(chunks):
    return [list(range(chunks))[i : i + chunks // 2] for i in (0, chunks // 2)]


def return_partials(acc_all, stat_all, side, peers):
    half = side // 2
    rows = acc_all.shape[2]
    tokens = rows // GROUP
    chunks = 4
    width = GROUP * HD
    groups = len(exchange_groups(chunks))
    message = (2, chunks, half, HD + 8, rows // chunks)
    return pl.pallas_call(
        functools.partial(return_kernel, side),
        out_shape=jax.ShapeDtypeStruct((tokens // peers, peers * width), jnp.bfloat16),
        in_specs=[VMEM] * 2,
        out_specs=HBM,
        scratch_shapes=[
            pltpu.VMEM(message, jnp.bfloat16),
            pltpu.VMEM(message, jnp.bfloat16),
            pltpu.VMEM((tokens, width), jnp.bfloat16),
            pltpu.SemaphoreType.DMA((2, chunks, half)),
            pltpu.SemaphoreType.DMA((2, chunks, half)),
            pltpu.SemaphoreType.DMA((groups, peers)),
            pltpu.SemaphoreType.DMA((groups, peers)),
            pltpu.SemaphoreType.DMA((groups,)),
        ],
        compiler_params=pltpu.CompilerParams(
            collective_id=1, has_side_effects=True, vmem_limit_bytes=16 << 20
        ),
        name="return_partials",
    )(acc_all, stat_all)


def per_device(
    queries,
    new_keys,
    new_values,
    library_keys,
    library_values,
    module_owner,
    module_page,
    module_count,
):
    rows_count = lax.axis_size("rows")
    peers = lax.axis_size("heads")
    side = math.isqrt(rows_count)
    k_all, v_all, q_all, table = gather_lines(
        module_owner, module_page, module_count, library_keys, library_values, queries, side
    )
    acc_all, stat_all = partials(table, q_all, new_keys, new_values, k_all, v_all, side)
    return return_partials(acc_all, stat_all, side, peers)


def solution(mesh):
    placed = (
        P("rows", "heads"),
        P("rows", "heads"),
        P("rows", "heads"),
        P("rows", None, "heads"),
        P("rows", None, "heads"),
        P("rows", None),
        P("rows", None),
        P("rows"),
    )
    return jax.shard_map(
        per_device,
        mesh=mesh,
        in_specs=placed,
        out_specs=P(("rows", "heads"), None),
        check_vma=False,
    )
```

```python
import functools
import math

import jax
import jax.numpy as jnp
from jax import lax
from jax.experimental import pallas as pl
from jax.experimental.pallas import tpu as pltpu
from jax.sharding import PartitionSpec as P

HD = 128
QH = 64
KVH = 8
GROUP = QH // KVH
MESH = pl.DeviceIdType.MESH
LOG2E = 1.4426950408889634
FLOOR = -1e30
NEAR_SLOTS = 3


def place(side):
    row = lax.axis_index("rows")
    core = lax.rem(lax.axis_index("heads"), 2)
    z, y = row // side, lax.rem(row, side)
    u = (1 - core) * z + core * y
    w = (1 - core) * y + core * z
    return core, u, w


def row_of(core, u, w, side):
    return (1 - core) * (u * side + w) + core * (w * side + u)


def wrap(value, side):
    return lax.rem(value + 4 * side, side)


def accumulate(acc, stat, q_all, req, keys, values, live=None, causal=False):
    scale = LOG2E / math.sqrt(HD)
    rows = q_all.shape[2]
    tokens = rows // GROUP
    wide = 2 * tokens
    for c in range(rows // wide):
        cols = slice(c * wide, (c + 1) * wide)
        raw = jnp.dot(keys, q_all[req, :, cols], preferred_element_type=jnp.float32)
        if causal:
            key_at = lax.broadcasted_iota(jnp.int32, raw.shape, 0)
            token_at = lax.rem(lax.broadcasted_iota(jnp.int32, raw.shape, 1), tokens)
            allowed = key_at <= token_at
            raw = jnp.where(allowed, raw, FLOOR)
        old = stat[req, 0:1, cols]
        high = jnp.max(raw, axis=0, keepdims=True) * scale
        if live is not None:
            high = jnp.where(live, high, FLOOR)
        top = jnp.maximum(old, high)
        base = top if live is None else jnp.where(live, top, -FLOOR)
        weights = jnp.exp2(raw * scale - base)
        if causal:
            weights = jnp.where(allowed, weights, 0.0)
        shrink = jnp.exp2(old - top)
        stat[req, 0:1, cols] = top
        stat[req, 1:2, cols] = stat[req, 1:2, cols] * shrink + jnp.sum(weights, axis=0, keepdims=True)
        mixed = jnp.dot(values, weights.astype(jnp.bfloat16), preferred_element_type=jnp.float32)
        acc[req, :, cols] = acc[req, :, cols] * shrink + mixed


def gather_kernel(
    side,
    owner_in, page_in, count, k_in, v_in, q_in, nk_in, nv_in,
    k_near, v_near, k_far, v_far, q_all, t_all, acc, stat,
    owner, page, table, vraw, qraw, nk, nv, send, recv, local,
):
    core, u, w = place(side)
    half = side // 2
    reach = k_near.shape[0] // 2
    heads_wide = q_all.shape[2] // 2
    shape = t_all.shape[1:]
    middle = shape[1] // 2
    slots = owner.shape[1]
    pages = k_in.shape[0]
    tokens = qraw.shape[0]
    lib_at = [row_of(core, wrap(u + d, side), w, side) for d in (1, -1)]
    que_at = [row_of(core, u, wrap(w + d, side), side) for d in (1, -1)]

    barrier = pltpu.get_barrier_semaphore()
    for row in lib_at + que_at:
        pl.semaphore_signal(barrier, inc=1, device_id={"rows": row}, device_id_type=MESH)

    def fetch(at, src, dst):
        copy = pltpu.make_async_copy(src, dst, local.at[at])
        copy.start()
        return copy

    lists = [fetch(0, owner_in, owner), fetch(1, page_in, page)]
    fetch_q, fetch_v = fetch(2, q_in, qraw), fetch(3, v_in, vraw)
    own_k = fetch(4, k_in, k_near.at[reach])
    fresh = [fetch(5, nk_in, nk), fetch(6, nv_in, nv)]
    pl.semaphore_wait(barrier, 4)

    def shard(kind, d):
        near, far = ((k_near, k_far), (v_near, v_far))[kind]
        if abs(d) <= reach:
            return near.at[d + reach]
        return far.at[d % side - reach - 1]

    started = {}
    waited = set()

    def receive(key):
        if key not in waited:
            started[key].wait_recv()
            waited.add(key)

    def start(dirn, step, kind):
        sign = (1, -1)[dirn]
        if step > 0:
            receive((dirn, step - 1, kind))
        if kind < 2:
            src = k_in if step == 0 and kind == 0 else shard(kind, -sign * step)
            dst, row = shard(kind, -sign * (step + 1)), lib_at[dirn]
        else:
            w0 = wrap(w - sign * step, side)
            dst, row = (q_all.at[w0], t_all.at[w0])[kind - 2], que_at[dirn]
            if kind == 2 and step == half - 1:
                dst = dst.at[:, pl.ds(dirn * heads_wide, heads_wide)]
            src = dst
        copy = pltpu.make_async_remote_copy(
            src_ref=src,
            dst_ref=dst,
            send_sem=send.at[dirn, step, kind],
            recv_sem=recv.at[dirn, step, kind],
            device_id={"rows": row},
            device_id_type=MESH,
        )
        copy.start()
        started[dirn, step, kind] = copy

    def both(step, kind):
        for dirn in (0, 1):
            start(dirn, step, kind)

    both(0, 0)
    for copy in lists:
        copy.wait()
    line_at = lax.broadcasted_iota(jnp.int32, shape, 0)
    lane_at = lax.broadcasted_iota(jnp.int32, shape, 1)
    filled = [jnp.zeros(shape, jnp.int32), jnp.full(shape, middle, jnp.int32)]
    packed = jnp.zeros(shape, jnp.int32)
    for slot in range(slots):
        z, y = owner[0, slot] // side, lax.rem(owner[0, slot], side)
        line = (1 - core) * z + core * y
        cross = (1 - core) * y + core * z
        ahead = wrap(line - u + reach, side)
        listed = jnp.logical_and(line_at == cross, count[0] > slot)
        for far in (0, 1):
            hit = jnp.logical_and(listed, (ahead > 2 * reach) if far else (ahead <= 2 * reach))
            spot = (ahead - far * (2 * reach + 1)) * pages + page[0, slot]
            packed = jnp.where(jnp.logical_and(hit, lane_at == filled[far]), spot, packed)
            filled[far] = filled[far] + jnp.where(hit, 1, 0)
    packed = jnp.where(lane_at == middle - 1, filled[0], packed)
    t_all[w] = jnp.where(lane_at == shape[1] - 1, filled[1] - middle, packed)
    both(0, 3)
    fetch_q.wait()
    for j in range(GROUP):
        q_all[w, :, j * tokens : (j + 1) * tokens] = jnp.transpose(qraw[:, j * HD : (j + 1) * HD])
    both(0, 2)
    fetch_v.wait()
    for j in range(pages):
        v_near[reach, j] = jnp.transpose(vraw[j])
    both(0, 1)
    for step in range(1, half - 1):
        both(step, 3)
    start(0, half - 1, 3)

    @pl.loop(0, side)
    def _(req):
        acc[req] = jnp.zeros(acc.shape[1:], jnp.float32)
        stat[req, 0:1] = jnp.full((1, acc.shape[2]), FLOOR, jnp.float32)
        stat[req, 1:2] = jnp.zeros((1, acc.shape[2]), jnp.float32)

    for copy in fresh:
        copy.wait()
    accumulate(acc, stat, q_all, w, nk[...], jnp.transpose(nv[...]), causal=True)
    receive((0, half - 1, 3))
    receive((1, half - 2, 3))
    to_scalars = fetch(7, t_all, table)

    both(1, 0)
    both(1, 2)
    both(1, 1)
    both(2, 2)
    both(2, 0)
    both(3, 2)
    both(2, 1)
    for dirn in (0, 1):
        receive((dirn, half - 1, 2))
    own_k.wait()
    to_scalars.wait()

    def listed_near(first, last):
        @pl.loop(first * NEAR_SLOTS, last * NEAR_SLOTS)
        def _(at):
            req, k = at // NEAR_SLOTS, lax.rem(at, NEAR_SLOTS)
            live = k < table[req, w, middle - 1]
            spot = table[req, w, k]
            line, page_at = spot // pages, lax.rem(spot, pages)
            accumulate(acc, stat, q_all, req, k_near[line, page_at], v_near[line, page_at], live=live)

    listed_near(0, half)
    start(0, half - 1, 0)
    start(1, half - 1, 1)
    listed_near(half, side)
    for key in started:
        receive(key)
    for copy in started.values():
        copy.wait_send()


HBM = pl.BlockSpec(memory_space=pltpu.HBM)
SMEM = pl.BlockSpec(memory_space=pltpu.SMEM)
VMEM = pl.BlockSpec(memory_space=pltpu.VMEM)


def in_hbm(a):
    return pltpu.with_memory_space_constraint(a, pltpu.HBM)


def gather_lines(owner, page, count, k, v, q, nk, nv, side):
    half = side // 2
    tokens = q.shape[0]
    near, far = 2 * (half - 2) + 1, side - 2 * (half - 2) - 1
    return pl.pallas_call(
        functools.partial(gather_kernel, side),
        out_shape=[
            pltpu.VMEM((near,) + k.shape, k.dtype),
            pltpu.VMEM((near,) + v.shape, v.dtype),
            pltpu.VMEM((far,) + k.shape, k.dtype),
            pltpu.VMEM((far,) + v.shape, v.dtype),
            pltpu.VMEM((side, HD, GROUP * tokens), q.dtype),
            pltpu.VMEM((side, side, 128), jnp.int32),
            pltpu.VMEM((side, HD, GROUP * tokens), jnp.float32),
            pltpu.VMEM((side, 2, GROUP * tokens), jnp.float32),
        ],
        in_specs=[HBM, HBM, SMEM] + [HBM] * 5,
        out_specs=[VMEM] * 8,
        scratch_shapes=[
            pltpu.SMEM(owner.shape, owner.dtype),
            pltpu.SMEM(page.shape, page.dtype),
            pltpu.SMEM((side, side, 128), jnp.int32),
            pltpu.VMEM(v.shape, v.dtype),
            pltpu.VMEM(q.shape, q.dtype),
            pltpu.VMEM(nk.shape, nk.dtype),
            pltpu.VMEM(nv.shape, nv.dtype),
            pltpu.SemaphoreType.DMA((2, half, 4)),
            pltpu.SemaphoreType.DMA((2, half, 4)),
            pltpu.SemaphoreType.DMA((8,)),
        ],
        compiler_params=pltpu.CompilerParams(
            collective_id=0, has_side_effects=True, vmem_limit_bytes=16 << 20
        ),
        name="gather_lines",
    )(in_hbm(owner), in_hbm(page), count, *[in_hbm(a) for a in (k, v, q, nk, nv)])


def partial_kernel(side, table, k_near, v_near, k_far, v_far, q_all, acc_in, stat_in, acc, stat):
    del acc_in, stat_in
    _, _, w = place(side)
    pages = k_near.shape[1]
    lanes = table.shape[2]
    middle = lanes // 2

    @pl.loop(0, side)
    def _(req):
        @pl.loop(NEAR_SLOTS, jnp.maximum(table[req, w, middle - 1], NEAR_SLOTS))
        def _(k):
            spot = table[req, w, k]
            line, page = spot // pages, lax.rem(spot, pages)
            accumulate(acc, stat, q_all, req, k_near[line, page], v_near[line, page])

        @pl.loop(0, table[req, w, lanes - 1])
        def _(k):
            spot = table[req, w, middle + k]
            line, page = spot // pages, lax.rem(spot, pages)
            accumulate(acc, stat, q_all, req, k_far[line, page], v_far[line, page])


def partials(table, k_near, v_near, k_far, v_far, q_all, acc, stat, side):
    return pl.pallas_call(
        functools.partial(partial_kernel, side),
        out_shape=[pltpu.VMEM(acc.shape, acc.dtype), pltpu.VMEM(stat.shape, stat.dtype)],
        in_specs=[SMEM] + [VMEM] * 7,
        out_specs=[VMEM, VMEM],
        input_output_aliases={6: 0, 7: 1},
        compiler_params=pltpu.CompilerParams(vmem_limit_bytes=16 << 20),
        name="partials",
    )(table, k_near, v_near, k_far, v_far, q_all, acc, stat)


def return_kernel(side, accs, stats, out, outgoing, incoming, result, send, recv, xsend, xrecv, xlocal):
    core, u, w = place(side)
    me = lax.axis_index("heads")
    peers = lax.axis_size("heads")
    half = side // 2
    chunks = outgoing.shape[1]
    part = outgoing.shape[4]
    extra = outgoing.shape[3] - HD
    tokens, width = result.shape
    share = tokens // peers
    near = [row_of(core, u, wrap(w + d, side), side) for d in (1, -1)]

    barrier = pltpu.get_barrier_semaphore()
    for row in near:
        pl.semaphore_signal(barrier, inc=1, device_id={"rows": row}, device_id_type=MESH)
    for hop in range(1, peers):
        pl.semaphore_signal(
            barrier, inc=1, device_id={"heads": lax.rem(me + hop, peers)}, device_id_type=MESH
        )

    def far(dirn, c):
        return half if c % 2 == dirn else half - 1

    def mine(d, c):
        target, cols = wrap(w + d, side), slice(c * part, (c + 1) * part)
        return accs[target, :, cols], stats[target, 0:1, cols], stats[target, 1:2, cols]

    def split(value):
        pieces = []
        for _ in range(3):
            pieces.append(value.astype(jnp.bfloat16).astype(jnp.float32))
            value = value - pieces[-1]
        return pieces

    row_at = lax.broadcasted_iota(jnp.int32, (extra, part), 0)

    def pack(ref, item):
        acc, top, total = item
        ref[0:HD] = acc.astype(jnp.bfloat16)
        tail = jnp.zeros((extra, part), jnp.float32)
        for i, piece in enumerate(split(top) + split(total)):
            tail = jnp.where(row_at == i, piece, tail)
        ref[HD : HD + extra] = tail.astype(jnp.bfloat16)

    def unpack(ref):
        tail = ref[HD : HD + extra].astype(jnp.float32)
        top = tail[0:1] + tail[1:2] + tail[2:3]
        total = tail[3:4] + tail[4:5] + tail[5:6]
        return ref[0:HD].astype(jnp.float32), top, total

    def merge(one, two):
        top = jnp.maximum(one[1], two[1])
        fa, fb = jnp.exp2(one[1] - top), jnp.exp2(two[1] - top)
        return one[0] * fa + two[0] * fb, top, one[2] * fa + two[2] * fb

    flights = {}

    def launch(dirn, c, k):
        copy = pltpu.make_async_remote_copy(
            src_ref=outgoing.at[dirn, c, k],
            dst_ref=incoming.at[dirn, c, k],
            send_sem=send.at[dirn, c, k],
            recv_sem=recv.at[dirn, c, k],
            device_id={"rows": near[dirn]},
            device_id_type=MESH,
        )
        copy.start()
        flights[dirn, c, k] = copy

    def arrived(dirn, c, k):
        flights[dirn, c, k].wait_recv()
        return unpack(incoming.at[dirn, c, k])

    starts = [(c, dirn) for c in range(chunks) for dirn in (0, 1)]
    for c, dirn in starts:
        pack(outgoing.at[dirn, c, 0], mine((1, -1)[dirn] * far(dirn, c), c))
    pl.semaphore_wait(barrier, 1 + peers)
    for c, dirn in starts:
        launch(dirn, c, 0)
    for k in range(1, half):
        for c, dirn in starts:
            reach = far(dirn, c) - k
            if reach < 1:
                continue
            item = mine((1, -1)[dirn] * reach, c)
            pack(outgoing.at[dirn, c, k], merge(item, arrived(dirn, c, k - 1)))
            launch(dirn, c, k)

    exchange = []
    groups = exchange_groups(chunks)
    for g, group in enumerate(groups):
        for c in group:
            item = mine(0, c)
            for dirn in sorted((0, 1), key=lambda dirn: far(dirn, c)):
                item = merge(item, arrived(dirn, c, far(dirn, c) - 1))
            final = item[0] / item[2]
            for j in range(part // tokens):
                at = c * part // tokens + j
                block = jnp.transpose(final[:, j * tokens : (j + 1) * tokens])
                result[:, at * HD : (at + 1) * HD] = block.astype(result.dtype)
        first, size = group[0] * part, len(group) * part
        here = slice(first, first + size)
        there = pl.ds(pl.multiple_of(me * width + first, size), size)
        for hop in range(1, peers):
            peer = lax.rem(me + hop, peers)
            copy = pltpu.make_async_remote_copy(
                src_ref=result.at[pl.ds(pl.multiple_of(peer * share, share), share), here],
                dst_ref=out.at[:, there],
                send_sem=xsend.at[g, hop],
                recv_sem=xrecv.at[g, hop],
                device_id={"heads": peer},
                device_id_type=MESH,
            )
            copy.start()
            exchange.append(copy)
        keep = pltpu.make_async_copy(
            result.at[pl.ds(pl.multiple_of(me * share, share), share), here], out.at[:, there], xlocal.at[g]
        )
        keep.start()
        exchange.append(keep)
    for copy in exchange:
        copy.wait()
    for copy in flights.values():
        copy.wait_send()


def exchange_groups(chunks):
    return [list(range(chunks))[i : i + chunks // 2] for i in (0, chunks // 2)]


def return_partials(acc_all, stat_all, side, peers):
    half = side // 2
    rows = acc_all.shape[2]
    tokens = rows // GROUP
    chunks = 4
    width = GROUP * HD
    groups = len(exchange_groups(chunks))
    message = (2, chunks, half, HD + 8, rows // chunks)
    return pl.pallas_call(
        functools.partial(return_kernel, side),
        out_shape=jax.ShapeDtypeStruct((tokens // peers, peers * width), jnp.bfloat16),
        in_specs=[VMEM] * 2,
        out_specs=HBM,
        scratch_shapes=[
            pltpu.VMEM(message, jnp.bfloat16),
            pltpu.VMEM(message, jnp.bfloat16),
            pltpu.VMEM((tokens, width), jnp.bfloat16),
            pltpu.SemaphoreType.DMA((2, chunks, half)),
            pltpu.SemaphoreType.DMA((2, chunks, half)),
            pltpu.SemaphoreType.DMA((groups, peers)),
            pltpu.SemaphoreType.DMA((groups, peers)),
            pltpu.SemaphoreType.DMA((groups,)),
        ],
        compiler_params=pltpu.CompilerParams(
            collective_id=1, has_side_effects=True, vmem_limit_bytes=16 << 20
        ),
        name="return_partials",
    )(acc_all, stat_all)


def per_device(
    queries,
    new_keys,
    new_values,
    library_keys,
    library_values,
    module_owner,
    module_page,
    module_count,
):
    rows_count = lax.axis_size("rows")
    peers = lax.axis_size("heads")
    side = math.isqrt(rows_count)
    *shards, q_all, table, acc, stat = gather_lines(
        module_owner,
        module_page,
        module_count,
        library_keys,
        library_values,
        queries,
        new_keys,
        new_values,
        side,
    )
    acc_all, stat_all = partials(table, *shards, q_all, acc, stat, side)
    return return_partials(acc_all, stat_all, side, peers)


def solution(mesh):
    placed = (
        P("rows", "heads"),
        P("rows", "heads"),
        P("rows", "heads"),
        P("rows", None, "heads"),
        P("rows", None, "heads"),
        P("rows", None),
        P("rows", None),
        P("rows"),
    )
    return jax.shard_map(
        per_device,
        mesh=mesh,
        in_specs=placed,
        out_specs=P(("rows", "heads"), None),
        check_vma=False,
    )
```

```python
import functools
import math

import jax
import jax.numpy as jnp
from jax import lax
from jax.experimental import pallas as pl
from jax.experimental.pallas import tpu as pltpu
from jax.sharding import PartitionSpec as P

HD = 128
QH = 64
KVH = 8
GROUP = QH // KVH
MESH = pl.DeviceIdType.MESH
LOG2E = 1.4426950408889634
FLOOR = -1e30
NEAR_SLOTS = 3
MID_SLOTS = 2
UNROLL = True


def place(side):
    row = lax.axis_index("rows")
    core = lax.rem(lax.axis_index("heads"), 2)
    z, y = row // side, lax.rem(row, side)
    u = (1 - core) * z + core * y
    w = (1 - core) * y + core * z
    return core, u, w


def row_of(core, u, w, side):
    return (1 - core) * (u * side + w) + core * (w * side + u)


def wrap(value, side):
    return lax.rem(value + 4 * side, side)


def accumulate(acc, stat, q_all, req, items, causal=False):
    scale = LOG2E / math.sqrt(HD)
    rows = q_all.shape[2]
    tokens = rows // GROUP
    wide = 2 * tokens
    for c in range(rows // wide):
        cols = slice(c * wide, (c + 1) * wide)
        query = q_all[req, :, cols]
        raws = [jnp.dot(keys, query, preferred_element_type=jnp.float32) for keys, _, _ in items]
        if causal:
            key_at = lax.broadcasted_iota(jnp.int32, raws[0].shape, 0)
            token_at = lax.rem(lax.broadcasted_iota(jnp.int32, raws[0].shape, 1), tokens)
            allowed = key_at <= token_at
            raws = [jnp.where(allowed, raw, FLOOR) for raw in raws]
        old = stat[req, 0:1, cols]
        top = old
        for raw, (_, _, live) in zip(raws, items):
            high = jnp.max(raw, axis=0, keepdims=True) * scale
            top = jnp.maximum(top, high if live is None else jnp.where(live, high, FLOOR))
        shrink = jnp.exp2(old - top)
        total = stat[req, 1:2, cols] * shrink
        mixed = acc[req, :, cols] * shrink
        for raw, (_, values, live) in zip(raws, items):
            base = top if live is None else jnp.where(live, top, -FLOOR)
            weights = jnp.exp2(raw * scale - base)
            if causal:
                weights = jnp.where(allowed, weights, 0.0)
            total = total + jnp.sum(weights, axis=0, keepdims=True)
            mixed = mixed + jnp.dot(values, weights.astype(jnp.bfloat16), preferred_element_type=jnp.float32)
        stat[req, 0:1, cols] = top
        stat[req, 1:2, cols] = total
        acc[req, :, cols] = mixed


def gather_kernel(
    side,
    owner_in, page_in, count, k_in, v_in, q_in, nk_in, nv_in,
    k_near, v_near, k_mid, v_mid, k_far, v_far, q_all, t_all, acc, stat,
    owner, page, table, vraw, qraw, nk, nv, send, recv, local,
):
    core, u, w = place(side)
    half = side // 2
    reach = k_near.shape[0] // 2
    heads_wide = q_all.shape[2] // 2
    shape = t_all.shape[1:]
    lanes = shape[1] // 4
    slots = owner.shape[1]
    pages = k_in.shape[0]
    tokens = qraw.shape[0]
    lib_at = [row_of(core, wrap(u + d, side), w, side) for d in (1, -1)]
    que_at = [row_of(core, u, wrap(w + d, side), side) for d in (1, -1)]

    barrier = pltpu.get_barrier_semaphore()
    for row in lib_at + que_at:
        pl.semaphore_signal(barrier, inc=1, device_id={"rows": row}, device_id_type=MESH)

    def fetch(at, src, dst):
        copy = pltpu.make_async_copy(src, dst, local.at[at])
        copy.start()
        return copy

    lists = [fetch(0, owner_in, owner), fetch(1, page_in, page)]
    fetch_q, fetch_v = fetch(2, q_in, qraw), fetch(3, v_in, vraw)
    own_k = fetch(4, k_in, k_near.at[reach])
    fresh = [fetch(5, nk_in, nk), fetch(6, nv_in, nv)]
    pl.semaphore_wait(barrier, 4)

    def shard(kind, d):
        near, mid, far = ((k_near, k_mid, k_far), (v_near, v_mid, v_far))[kind]
        if abs(d) <= reach:
            return near.at[d + reach]
        return far.at[0] if abs(d) == half else mid.at[(reach - d) // side + 1]

    started = {}
    waited = set()

    def receive(key):
        if key not in waited:
            started[key].wait_recv()
            waited.add(key)

    def start(dirn, step, kind):
        sign = (1, -1)[dirn]
        if step > 0:
            receive((dirn, step - 1, kind))
        if kind < 2:
            src = k_in if step == 0 and kind == 0 else shard(kind, -sign * step)
            dst, row = shard(kind, -sign * (step + 1)), lib_at[dirn]
        else:
            w0 = wrap(w - sign * step, side)
            dst, row = (q_all.at[w0], t_all.at[w0])[kind - 2], que_at[dirn]
            if kind == 2 and step == half - 1:
                dst = dst.at[:, pl.ds(dirn * heads_wide, heads_wide)]
            src = dst
        copy = pltpu.make_async_remote_copy(
            src_ref=src,
            dst_ref=dst,
            send_sem=send.at[dirn, step, kind],
            recv_sem=recv.at[dirn, step, kind],
            device_id={"rows": row},
            device_id_type=MESH,
        )
        copy.start()
        started[dirn, step, kind] = copy

    def both(step, kind):
        for dirn in (0, 1):
            start(dirn, step, kind)

    both(0, 0)
    for copy in lists:
        copy.wait()
    line_at = lax.broadcasted_iota(jnp.int32, shape, 0)
    lane_at = lax.broadcasted_iota(jnp.int32, shape, 1)
    filled = [jnp.full(shape, g * lanes, jnp.int32) for g in range(3)]
    packed = jnp.zeros(shape, jnp.int32)
    for slot in range(slots):
        z, y = owner[0, slot] // side, lax.rem(owner[0, slot], side)
        line = (1 - core) * z + core * y
        cross = (1 - core) * y + core * z
        ahead = wrap(line - u + reach, side)
        listed = jnp.logical_and(line_at == cross, count[0] > slot)
        beyond = ahead - 2 * reach - 1
        groups = (
            (beyond < 0, ahead),
            (jnp.logical_or(beyond == 0, beyond == 2), beyond // 2),
            (beyond == 1, 0),
        )
        for g, (belongs, shard_at) in enumerate(groups):
            hit = jnp.logical_and(listed, belongs)
            spot = shard_at * pages + page[0, slot]
            packed = jnp.where(jnp.logical_and(hit, lane_at == filled[g]), spot, packed)
            filled[g] = filled[g] + jnp.where(hit, 1, 0)
    for g in range(3):
        packed = jnp.where(lane_at == (g + 1) * lanes - 1, filled[g] - g * lanes, packed)
    t_all[w] = packed
    both(0, 3)
    fetch_q.wait()
    for j in range(GROUP):
        q_all[w, :, j * tokens : (j + 1) * tokens] = jnp.transpose(qraw[:, j * HD : (j + 1) * HD])
    both(0, 2)
    fetch_v.wait()
    for j in range(pages):
        v_near[reach, j] = jnp.transpose(vraw[j])
    both(0, 1)
    for step in range(1, half - 1):
        both(step, 3)
    start(0, half - 1, 3)

    @pl.loop(0, side)
    def _(req):
        acc[req] = jnp.zeros(acc.shape[1:], jnp.float32)
        stat[req, 0:1] = jnp.full((1, acc.shape[2]), FLOOR, jnp.float32)
        stat[req, 1:2] = jnp.zeros((1, acc.shape[2]), jnp.float32)

    for copy in fresh:
        copy.wait()
    accumulate(acc, stat, q_all, w, [(nk[...], jnp.transpose(nv[...]), None)], causal=True)
    receive((0, half - 1, 3))
    receive((1, half - 2, 3))
    to_scalars = fetch(7, t_all, table)

    both(1, 0)
    both(1, 2)
    both(1, 1)
    both(2, 2)
    both(2, 0)
    both(3, 2)
    both(2, 1)
    for dirn in (0, 1):
        receive((dirn, half - 1, 2))
    own_k.wait()
    to_scalars.wait()

    def listed(g, most, first, last, keys, values):
        def one(req):
            items = []
            for k in range(most):
                live = k < table[req, w, (g + 1) * lanes - 1]
                spot = table[req, w, g * lanes + k]
                shard_at, page_at = spot // pages, lax.rem(spot, pages)
                items.append((keys[shard_at, page_at], values[shard_at, page_at], live))
            accumulate(acc, stat, q_all, req, items)

        if UNROLL:
            for req in range(first, last):
                one(req)
        else:
            pl.loop(first, last)(one)

    listed(0, NEAR_SLOTS, 0, half, k_near, v_near)
    start(0, half - 1, 0)
    start(1, half - 1, 1)
    listed(0, NEAR_SLOTS, half, side, k_near, v_near)
    for dirn in (0, 1):
        for kind in (0, 1):
            receive((dirn, half - 2, kind))
    listed(1, MID_SLOTS, 0, side, k_mid, v_mid)
    for key in started:
        receive(key)
    for copy in started.values():
        copy.wait_send()


HBM = pl.BlockSpec(memory_space=pltpu.HBM)
SMEM = pl.BlockSpec(memory_space=pltpu.SMEM)
VMEM = pl.BlockSpec(memory_space=pltpu.VMEM)


def in_hbm(a):
    return pltpu.with_memory_space_constraint(a, pltpu.HBM)


def gather_lines(owner, page, count, k, v, q, nk, nv, side):
    half = side // 2
    tokens = q.shape[0]
    near = 2 * (half - 2) + 1
    return pl.pallas_call(
        functools.partial(gather_kernel, side),
        out_shape=[
            *[pltpu.VMEM((n,) + a.shape, a.dtype) for n in (near, 2, 1) for a in (k, v)],
            pltpu.VMEM((side, HD, GROUP * tokens), q.dtype),
            pltpu.VMEM((side, side, 128), jnp.int32),
            pltpu.VMEM((side, HD, GROUP * tokens), jnp.float32),
            pltpu.VMEM((side, 2, GROUP * tokens), jnp.float32),
        ],
        in_specs=[HBM, HBM, SMEM] + [HBM] * 5,
        out_specs=[VMEM] * 10,
        scratch_shapes=[
            pltpu.SMEM(owner.shape, owner.dtype),
            pltpu.SMEM(page.shape, page.dtype),
            pltpu.SMEM((side, side, 128), jnp.int32),
            pltpu.VMEM(v.shape, v.dtype),
            pltpu.VMEM(q.shape, q.dtype),
            pltpu.VMEM(nk.shape, nk.dtype),
            pltpu.VMEM(nv.shape, nv.dtype),
            pltpu.SemaphoreType.DMA((2, half, 4)),
            pltpu.SemaphoreType.DMA((2, half, 4)),
            pltpu.SemaphoreType.DMA((8,)),
        ],
        compiler_params=pltpu.CompilerParams(
            collective_id=0, has_side_effects=True, vmem_limit_bytes=16 << 20
        ),
        name="gather_lines",
    )(in_hbm(owner), in_hbm(page), count, *[in_hbm(a) for a in (k, v, q, nk, nv)])


def partial_kernel(side, table, *refs):
    shards, (q_all, _, _, acc, stat) = refs[:-5], refs[-5:]
    _, _, w = place(side)
    pages = shards[0].shape[1]
    lanes = table.shape[2] // 4

    @pl.loop(0, side)
    def _(req):
        for g, done in enumerate((NEAR_SLOTS, MID_SLOTS, 0)):
            keys, values = shards[2 * g], shards[2 * g + 1]

            @pl.loop(done, jnp.maximum(table[req, w, (g + 1) * lanes - 1], done))
            def _(k):
                spot = table[req, w, g * lanes + k]
                shard_at, page_at = spot // pages, lax.rem(spot, pages)
                accumulate(acc, stat, q_all, req, [(keys[shard_at, page_at], values[shard_at, page_at], None)])


def partials(table, shards, q_all, acc, stat, side):
    first = 2 + len(shards)
    return pl.pallas_call(
        functools.partial(partial_kernel, side),
        out_shape=[pltpu.VMEM(acc.shape, acc.dtype), pltpu.VMEM(stat.shape, stat.dtype)],
        in_specs=[SMEM] + [VMEM] * (first + 1),
        out_specs=[VMEM, VMEM],
        input_output_aliases={first: 0, first + 1: 1},
        compiler_params=pltpu.CompilerParams(vmem_limit_bytes=16 << 20),
        name="partials",
    )(table, *shards, q_all, acc, stat)


def return_kernel(side, accs, stats, out, outgoing, incoming, result, send, recv, xsend, xrecv, xlocal):
    core, u, w = place(side)
    me = lax.axis_index("heads")
    peers = lax.axis_size("heads")
    half = side // 2
    chunks = outgoing.shape[1]
    part = outgoing.shape[4]
    extra = outgoing.shape[3] - HD
    tokens, width = result.shape
    share = tokens // peers
    near = [row_of(core, u, wrap(w + d, side), side) for d in (1, -1)]

    barrier = pltpu.get_barrier_semaphore()
    for row in near:
        pl.semaphore_signal(barrier, inc=1, device_id={"rows": row}, device_id_type=MESH)
    for hop in range(1, peers):
        pl.semaphore_signal(
            barrier, inc=1, device_id={"heads": lax.rem(me + hop, peers)}, device_id_type=MESH
        )

    def far(dirn, c):
        return half if c % 2 == dirn else half - 1

    def mine(d, c):
        target, cols = wrap(w + d, side), slice(c * part, (c + 1) * part)
        return accs[target, :, cols], stats[target, 0:1, cols], stats[target, 1:2, cols]

    def split(value):
        pieces = []
        for _ in range(3):
            pieces.append(value.astype(jnp.bfloat16).astype(jnp.float32))
            value = value - pieces[-1]
        return pieces

    row_at = lax.broadcasted_iota(jnp.int32, (extra, part), 0)

    def pack(ref, item):
        acc, top, total = item
        ref[0:HD] = acc.astype(jnp.bfloat16)
        tail = jnp.zeros((extra, part), jnp.float32)
        for i, piece in enumerate(split(top) + split(total)):
            tail = jnp.where(row_at == i, piece, tail)
        ref[HD : HD + extra] = tail.astype(jnp.bfloat16)

    def unpack(ref):
        tail = ref[HD : HD + extra].astype(jnp.float32)
        top = tail[0:1] + tail[1:2] + tail[2:3]
        total = tail[3:4] + tail[4:5] + tail[5:6]
        return ref[0:HD].astype(jnp.float32), top, total

    def merge(one, two):
        top = jnp.maximum(one[1], two[1])
        fa, fb = jnp.exp2(one[1] - top), jnp.exp2(two[1] - top)
        return one[0] * fa + two[0] * fb, top, one[2] * fa + two[2] * fb

    flights = {}

    def launch(dirn, c, k):
        copy = pltpu.make_async_remote_copy(
            src_ref=outgoing.at[dirn, c, k],
            dst_ref=incoming.at[dirn, c, k],
            send_sem=send.at[dirn, c, k],
            recv_sem=recv.at[dirn, c, k],
            device_id={"rows": near[dirn]},
            device_id_type=MESH,
        )
        copy.start()
        flights[dirn, c, k] = copy

    def arrived(dirn, c, k):
        flights[dirn, c, k].wait_recv()
        return unpack(incoming.at[dirn, c, k])

    starts = [(c, dirn) for c in range(chunks) for dirn in (0, 1)]
    for c, dirn in starts:
        pack(outgoing.at[dirn, c, 0], mine((1, -1)[dirn] * far(dirn, c), c))
    pl.semaphore_wait(barrier, 1 + peers)
    for c, dirn in starts:
        launch(dirn, c, 0)
    for k in range(1, half):
        for c, dirn in starts:
            reach = far(dirn, c) - k
            if reach < 1:
                continue
            item = mine((1, -1)[dirn] * reach, c)
            pack(outgoing.at[dirn, c, k], merge(item, arrived(dirn, c, k - 1)))
            launch(dirn, c, k)

    exchange = []
    groups = exchange_groups(chunks)
    for g, group in enumerate(groups):
        for c in group:
            item = mine(0, c)
            for dirn in sorted((0, 1), key=lambda dirn: far(dirn, c)):
                item = merge(item, arrived(dirn, c, far(dirn, c) - 1))
            final = item[0] / item[2]
            for j in range(part // tokens):
                at = c * part // tokens + j
                block = jnp.transpose(final[:, j * tokens : (j + 1) * tokens])
                result[:, at * HD : (at + 1) * HD] = block.astype(result.dtype)
        first, size = group[0] * part, len(group) * part
        here = slice(first, first + size)
        there = pl.ds(pl.multiple_of(me * width + first, size), size)
        for hop in range(1, peers):
            peer = lax.rem(me + hop, peers)
            copy = pltpu.make_async_remote_copy(
                src_ref=result.at[pl.ds(pl.multiple_of(peer * share, share), share), here],
                dst_ref=out.at[:, there],
                send_sem=xsend.at[g, hop],
                recv_sem=xrecv.at[g, hop],
                device_id={"heads": peer},
                device_id_type=MESH,
            )
            copy.start()
            exchange.append(copy)
        keep = pltpu.make_async_copy(
            result.at[pl.ds(pl.multiple_of(me * share, share), share), here], out.at[:, there], xlocal.at[g]
        )
        keep.start()
        exchange.append(keep)
    for copy in exchange:
        copy.wait()
    for copy in flights.values():
        copy.wait_send()


def exchange_groups(chunks):
    return [list(range(chunks))[i : i + chunks // 2] for i in (0, chunks // 2)]


def return_partials(acc_all, stat_all, side, peers):
    half = side // 2
    rows = acc_all.shape[2]
    tokens = rows // GROUP
    chunks = 4
    width = GROUP * HD
    groups = len(exchange_groups(chunks))
    message = (2, chunks, half, HD + 8, rows // chunks)
    return pl.pallas_call(
        functools.partial(return_kernel, side),
        out_shape=jax.ShapeDtypeStruct((tokens // peers, peers * width), jnp.bfloat16),
        in_specs=[VMEM] * 2,
        out_specs=HBM,
        scratch_shapes=[
            pltpu.VMEM(message, jnp.bfloat16),
            pltpu.VMEM(message, jnp.bfloat16),
            pltpu.VMEM((tokens, width), jnp.bfloat16),
            pltpu.SemaphoreType.DMA((2, chunks, half)),
            pltpu.SemaphoreType.DMA((2, chunks, half)),
            pltpu.SemaphoreType.DMA((groups, peers)),
            pltpu.SemaphoreType.DMA((groups, peers)),
            pltpu.SemaphoreType.DMA((groups,)),
        ],
        compiler_params=pltpu.CompilerParams(
            collective_id=1, has_side_effects=True, vmem_limit_bytes=16 << 20
        ),
        name="return_partials",
    )(acc_all, stat_all)


def per_device(
    queries,
    new_keys,
    new_values,
    library_keys,
    library_values,
    module_owner,
    module_page,
    module_count,
):
    rows_count = lax.axis_size("rows")
    peers = lax.axis_size("heads")
    side = math.isqrt(rows_count)
    *shards, q_all, table, acc, stat = gather_lines(
        module_owner,
        module_page,
        module_count,
        library_keys,
        library_values,
        queries,
        new_keys,
        new_values,
        side,
    )
    acc_all, stat_all = partials(table, shards, q_all, acc, stat, side)
    return return_partials(acc_all, stat_all, side, peers)


def solution(mesh):
    placed = (
        P("rows", "heads"),
        P("rows", "heads"),
        P("rows", "heads"),
        P("rows", None, "heads"),
        P("rows", None, "heads"),
        P("rows", None),
        P("rows", None),
        P("rows"),
    )
    return jax.shard_map(
        per_device,
        mesh=mesh,
        in_specs=placed,
        out_specs=P(("rows", "heads"), None),
        check_vma=False,
    )
```

```python
import functools
import math

import jax
import jax.numpy as jnp
from jax import lax
from jax.experimental import pallas as pl
from jax.experimental.pallas import tpu as pltpu
from jax.sharding import PartitionSpec as P

HD = 128
QH = 64
KVH = 8
GROUP = QH // KVH
MESH = pl.DeviceIdType.MESH
LOG2E = 1.4426950408889634
FLOOR = -1e30
NEAR_SLOTS = 4
MID_SLOTS = 2
UNROLL = True


def place(side):
    row = lax.axis_index("rows")
    core = lax.rem(lax.axis_index("heads"), 2)
    z, y = row // side, lax.rem(row, side)
    u = (1 - core) * z + core * y
    w = (1 - core) * y + core * z
    return core, u, w


def row_of(core, u, w, side):
    return (1 - core) * (u * side + w) + core * (w * side + u)


def wrap(value, side):
    return lax.rem(value + 4 * side, side)


def accumulate(acc, stat, q_all, req, items, causal=False):
    scale = LOG2E / math.sqrt(HD)
    rows = q_all.shape[2]
    tokens = rows // GROUP
    wide = 2 * tokens
    for c in range(rows // wide):
        cols = slice(c * wide, (c + 1) * wide)
        query = q_all[req, :, cols]
        raws = [jnp.dot(keys, query, preferred_element_type=jnp.float32) for keys, _, _ in items]
        if causal:
            key_at = lax.broadcasted_iota(jnp.int32, raws[0].shape, 0)
            token_at = lax.rem(lax.broadcasted_iota(jnp.int32, raws[0].shape, 1), tokens)
            allowed = key_at <= token_at
            raws = [jnp.where(allowed, raw, FLOOR) for raw in raws]
        old = stat[req, 0:1, cols]
        top = old
        for raw, (_, _, live) in zip(raws, items):
            high = jnp.max(raw, axis=0, keepdims=True) * scale
            top = jnp.maximum(top, high if live is None else jnp.where(live, high, FLOOR))
        shrink = jnp.exp2(old - top)
        total = stat[req, 1:2, cols] * shrink
        mixed = acc[req, :, cols] * shrink
        for raw, (_, values, live) in zip(raws, items):
            base = top if live is None else jnp.where(live, top, -FLOOR)
            weights = jnp.exp2(raw * scale - base)
            if causal:
                weights = jnp.where(allowed, weights, 0.0)
            total = total + jnp.sum(weights, axis=0, keepdims=True)
            mixed = mixed + jnp.dot(values, weights.astype(jnp.bfloat16), preferred_element_type=jnp.float32)
        stat[req, 0:1, cols] = top
        stat[req, 1:2, cols] = total
        acc[req, :, cols] = mixed


def gather_kernel(
    side,
    owner_in, page_in, count, k_in, v_in, q_in, nk_in, nv_in,
    k_near, v_near, k_mid, v_mid, k_far, v_far, q_all, t_all, acc, stat,
    owner, page, table, vraw, qraw, nk, nv, send, recv, local,
):
    core, u, w = place(side)
    half = side // 2
    reach = k_near.shape[0] // 2
    heads_wide = q_all.shape[2] // 2
    shape = t_all.shape[1:]
    lanes = shape[1] // 4
    slots = owner.shape[1]
    pages = k_in.shape[0]
    tokens = qraw.shape[0]
    lib_at = [row_of(core, wrap(u + d, side), w, side) for d in (1, -1)]
    que_at = [row_of(core, u, wrap(w + d, side), side) for d in (1, -1)]

    barrier = pltpu.get_barrier_semaphore()
    for row in lib_at + que_at:
        pl.semaphore_signal(barrier, inc=1, device_id={"rows": row}, device_id_type=MESH)

    def fetch(at, src, dst):
        copy = pltpu.make_async_copy(src, dst, local.at[at])
        copy.start()
        return copy

    lists = [fetch(0, owner_in, owner), fetch(1, page_in, page)]
    fetch_q, fetch_v = fetch(2, q_in, qraw), fetch(3, v_in, vraw)
    own_k = fetch(4, k_in, k_near.at[reach])
    fresh = [fetch(5, nk_in, nk), fetch(6, nv_in, nv)]
    pl.semaphore_wait(barrier, 4)

    def shard(kind, d):
        near, mid, far = ((k_near, k_mid, k_far), (v_near, v_mid, v_far))[kind]
        if abs(d) <= reach:
            return near.at[d + reach]
        return far.at[0] if abs(d) == half else mid.at[(reach - d) // side + 1]

    started = {}
    waited = set()

    def receive(key):
        if key not in waited:
            started[key].wait_recv()
            waited.add(key)

    def start(dirn, step, kind):
        sign = (1, -1)[dirn]
        if step > 0:
            receive((dirn, step - 1, kind))
        if kind < 2:
            src = k_in if step == 0 and kind == 0 else shard(kind, -sign * step)
            dst, row = shard(kind, -sign * (step + 1)), lib_at[dirn]
        else:
            w0 = wrap(w - sign * step, side)
            dst, row = (q_all.at[w0], t_all.at[w0])[kind - 2], que_at[dirn]
            if kind == 2 and step == half - 1:
                dst = dst.at[:, pl.ds(dirn * heads_wide, heads_wide)]
            src = dst
        copy = pltpu.make_async_remote_copy(
            src_ref=src,
            dst_ref=dst,
            send_sem=send.at[dirn, step, kind],
            recv_sem=recv.at[dirn, step, kind],
            device_id={"rows": row},
            device_id_type=MESH,
        )
        copy.start()
        started[dirn, step, kind] = copy

    def both(step, kind):
        for dirn in (0, 1):
            start(dirn, step, kind)

    both(0, 0)
    for copy in lists:
        copy.wait()
    line_at = lax.broadcasted_iota(jnp.int32, shape, 0)
    lane_at = lax.broadcasted_iota(jnp.int32, shape, 1)
    filled = [jnp.full(shape, g * lanes, jnp.int32) for g in range(3)]
    packed = jnp.zeros(shape, jnp.int32)
    for slot in range(slots):
        z, y = owner[0, slot] // side, lax.rem(owner[0, slot], side)
        line = (1 - core) * z + core * y
        cross = (1 - core) * y + core * z
        ahead = wrap(line - u + reach, side)
        listed = jnp.logical_and(line_at == cross, count[0] > slot)
        beyond = ahead - 2 * reach - 1
        groups = (
            (beyond < 0, ahead),
            (jnp.logical_or(beyond == 0, beyond == 2), beyond // 2),
            (beyond == 1, 0),
        )
        for g, (belongs, shard_at) in enumerate(groups):
            hit = jnp.logical_and(listed, belongs)
            spot = shard_at * pages + page[0, slot]
            packed = jnp.where(jnp.logical_and(hit, lane_at == filled[g]), spot, packed)
            filled[g] = filled[g] + jnp.where(hit, 1, 0)
    for g in range(3):
        packed = jnp.where(lane_at == (g + 1) * lanes - 1, filled[g] - g * lanes, packed)
    t_all[w] = packed
    both(0, 3)
    fetch_q.wait()
    for j in range(GROUP):
        q_all[w, :, j * tokens : (j + 1) * tokens] = jnp.transpose(qraw[:, j * HD : (j + 1) * HD])
    both(0, 2)
    fetch_v.wait()
    for j in range(pages):
        v_near[reach, j] = jnp.transpose(vraw[j])
    both(0, 1)
    for step in range(1, half - 1):
        both(step, 3)
    start(0, half - 1, 3)

    @pl.loop(0, side)
    def _(req):
        acc[req] = jnp.zeros(acc.shape[1:], jnp.float32)
        stat[req, 0:1] = jnp.full((1, acc.shape[2]), FLOOR, jnp.float32)
        stat[req, 1:2] = jnp.zeros((1, acc.shape[2]), jnp.float32)

    for copy in fresh:
        copy.wait()
    accumulate(acc, stat, q_all, w, [(nk[...], jnp.transpose(nv[...]), None)], causal=True)
    receive((0, half - 1, 3))
    receive((1, half - 2, 3))
    to_scalars = fetch(7, t_all, table)

    both(1, 0)
    both(1, 2)
    both(1, 1)
    both(2, 2)
    both(2, 0)
    both(3, 2)
    both(2, 1)
    for dirn in (0, 1):
        receive((dirn, half - 1, 2))
    own_k.wait()
    to_scalars.wait()

    def listed(g, most, first, last, keys, values):
        def one(req):
            items = []
            for k in range(most):
                live = k < table[req, w, (g + 1) * lanes - 1]
                spot = table[req, w, g * lanes + k]
                shard_at, page_at = spot // pages, lax.rem(spot, pages)
                items.append((keys[shard_at, page_at], values[shard_at, page_at], live))
            accumulate(acc, stat, q_all, req, items)

        if UNROLL:
            for req in range(first, last):
                one(req)
        else:
            pl.loop(first, last)(one)

    listed(0, NEAR_SLOTS, 0, half, k_near, v_near)
    start(0, half - 1, 0)
    start(1, half - 1, 1)
    listed(0, NEAR_SLOTS, half, side, k_near, v_near)
    for dirn in (0, 1):
        for kind in (0, 1):
            receive((dirn, half - 2, kind))
    listed(1, MID_SLOTS, 0, side, k_mid, v_mid)
    for key in started:
        receive(key)
    for copy in started.values():
        copy.wait_send()


HBM = pl.BlockSpec(memory_space=pltpu.HBM)
SMEM = pl.BlockSpec(memory_space=pltpu.SMEM)
VMEM = pl.BlockSpec(memory_space=pltpu.VMEM)


def in_hbm(a):
    return pltpu.with_memory_space_constraint(a, pltpu.HBM)


def gather_lines(owner, page, count, k, v, q, nk, nv, side):
    half = side // 2
    tokens = q.shape[0]
    near = 2 * (half - 2) + 1
    return pl.pallas_call(
        functools.partial(gather_kernel, side),
        out_shape=[
            *[pltpu.VMEM((n,) + a.shape, a.dtype) for n in (near, 2, 1) for a in (k, v)],
            pltpu.VMEM((side, HD, GROUP * tokens), q.dtype),
            pltpu.VMEM((side, side, 128), jnp.int32),
            pltpu.VMEM((side, HD, GROUP * tokens), jnp.float32),
            pltpu.VMEM((side, 2, GROUP * tokens), jnp.float32),
        ],
        in_specs=[HBM, HBM, SMEM] + [HBM] * 5,
        out_specs=[VMEM] * 10,
        scratch_shapes=[
            pltpu.SMEM(owner.shape, owner.dtype),
            pltpu.SMEM(page.shape, page.dtype),
            pltpu.SMEM((side, side, 128), jnp.int32),
            pltpu.VMEM(v.shape, v.dtype),
            pltpu.VMEM(q.shape, q.dtype),
            pltpu.VMEM(nk.shape, nk.dtype),
            pltpu.VMEM(nv.shape, nv.dtype),
            pltpu.SemaphoreType.DMA((2, half, 4)),
            pltpu.SemaphoreType.DMA((2, half, 4)),
            pltpu.SemaphoreType.DMA((8,)),
        ],
        compiler_params=pltpu.CompilerParams(
            collective_id=0, has_side_effects=True, vmem_limit_bytes=16 << 20
        ),
        name="gather_lines",
    )(in_hbm(owner), in_hbm(page), count, *[in_hbm(a) for a in (k, v, q, nk, nv)])


def partial_kernel(side, table, *refs):
    shards, (q_all, _, _, acc, stat) = refs[:-5], refs[-5:]
    _, _, w = place(side)
    pages = shards[0].shape[1]
    lanes = table.shape[2] // 4

    @pl.loop(0, side)
    def _(req):
        for g, done in enumerate((NEAR_SLOTS, MID_SLOTS, 0)):
            keys, values = shards[2 * g], shards[2 * g + 1]

            @pl.loop(done, jnp.maximum(table[req, w, (g + 1) * lanes - 1], done))
            def _(k):
                spot = table[req, w, g * lanes + k]
                shard_at, page_at = spot // pages, lax.rem(spot, pages)
                accumulate(acc, stat, q_all, req, [(keys[shard_at, page_at], values[shard_at, page_at], None)])


def partials(table, shards, q_all, acc, stat, side):
    first = 2 + len(shards)
    return pl.pallas_call(
        functools.partial(partial_kernel, side),
        out_shape=[pltpu.VMEM(acc.shape, acc.dtype), pltpu.VMEM(stat.shape, stat.dtype)],
        in_specs=[SMEM] + [VMEM] * (first + 1),
        out_specs=[VMEM, VMEM],
        input_output_aliases={first: 0, first + 1: 1},
        compiler_params=pltpu.CompilerParams(vmem_limit_bytes=16 << 20),
        name="partials",
    )(table, *shards, q_all, acc, stat)


def return_kernel(side, accs, stats, out, outgoing, incoming, result, send, recv, xsend, xrecv, xlocal):
    core, u, w = place(side)
    me = lax.axis_index("heads")
    peers = lax.axis_size("heads")
    half = side // 2
    chunks = outgoing.shape[1]
    part = outgoing.shape[4]
    extra = outgoing.shape[3] - HD
    tokens, width = result.shape
    share = tokens // peers
    near = [row_of(core, u, wrap(w + d, side), side) for d in (1, -1)]

    barrier = pltpu.get_barrier_semaphore()
    for row in near:
        pl.semaphore_signal(barrier, inc=1, device_id={"rows": row}, device_id_type=MESH)
    for hop in range(1, peers):
        pl.semaphore_signal(
            barrier, inc=1, device_id={"heads": lax.rem(me + hop, peers)}, device_id_type=MESH
        )

    def far(dirn, c):
        return half if c % 2 == dirn else half - 1

    def mine(d, c):
        target, cols = wrap(w + d, side), slice(c * part, (c + 1) * part)
        return accs[target, :, cols], stats[target, 0:1, cols], stats[target, 1:2, cols]

    def split(value):
        pieces = []
        for _ in range(3):
            pieces.append(value.astype(jnp.bfloat16).astype(jnp.float32))
            value = value - pieces[-1]
        return pieces

    row_at = lax.broadcasted_iota(jnp.int32, (extra, part), 0)

    def pack(ref, item):
        acc, top, total = item
        ref[0:HD] = acc.astype(jnp.bfloat16)
        tail = jnp.zeros((extra, part), jnp.float32)
        for i, piece in enumerate(split(top) + split(total)):
            tail = jnp.where(row_at == i, piece, tail)
        ref[HD : HD + extra] = tail.astype(jnp.bfloat16)

    def unpack(ref):
        tail = ref[HD : HD + extra].astype(jnp.float32)
        top = tail[0:1] + tail[1:2] + tail[2:3]
        total = tail[3:4] + tail[4:5] + tail[5:6]
        return ref[0:HD].astype(jnp.float32), top, total

    def merge(one, two):
        top = jnp.maximum(one[1], two[1])
        fa, fb = jnp.exp2(one[1] - top), jnp.exp2(two[1] - top)
        return one[0] * fa + two[0] * fb, top, one[2] * fa + two[2] * fb

    flights = {}

    def launch(dirn, c, k):
        copy = pltpu.make_async_remote_copy(
            src_ref=outgoing.at[dirn, c, k],
            dst_ref=incoming.at[dirn, c, k],
            send_sem=send.at[dirn, c, k],
            recv_sem=recv.at[dirn, c, k],
            device_id={"rows": near[dirn]},
            device_id_type=MESH,
        )
        copy.start()
        flights[dirn, c, k] = copy

    def arrived(dirn, c, k):
        flights[dirn, c, k].wait_recv()
        return unpack(incoming.at[dirn, c, k])

    starts = [(c, dirn) for c in range(chunks) for dirn in (0, 1)]
    for c, dirn in starts:
        pack(outgoing.at[dirn, c, 0], mine((1, -1)[dirn] * far(dirn, c), c))
    pl.semaphore_wait(barrier, 1 + peers)
    for c, dirn in starts:
        launch(dirn, c, 0)
    for k in range(1, half):
        for c, dirn in starts:
            reach = far(dirn, c) - k
            if reach < 1:
                continue
            item = mine((1, -1)[dirn] * reach, c)
            pack(outgoing.at[dirn, c, k], merge(item, arrived(dirn, c, k - 1)))
            launch(dirn, c, k)

    exchange = []
    groups = exchange_groups(chunks)
    for g, group in enumerate(groups):
        for c in group:
            item = mine(0, c)
            for dirn in sorted((0, 1), key=lambda dirn: far(dirn, c)):
                item = merge(item, arrived(dirn, c, far(dirn, c) - 1))
            final = item[0] / item[2]
            for j in range(part // tokens):
                at = c * part // tokens + j
                block = jnp.transpose(final[:, j * tokens : (j + 1) * tokens].astype(result.dtype))
                result[:, at * HD : (at + 1) * HD] = block
        first, size = group[0] * part, len(group) * part
        here = slice(first, first + size)
        there = pl.ds(pl.multiple_of(me * width + first, size), size)
        for hop in sorted(range(1, peers), key=lambda hop: abs(hop - peers // 2)):
            peer = lax.rem(me + hop, peers)
            copy = pltpu.make_async_remote_copy(
                src_ref=result.at[pl.ds(pl.multiple_of(peer * share, share), share), here],
                dst_ref=out.at[:, there],
                send_sem=xsend.at[g, hop],
                recv_sem=xrecv.at[g, hop],
                device_id={"heads": peer},
                device_id_type=MESH,
            )
            copy.start()
            exchange.append(copy)
        keep = pltpu.make_async_copy(
            result.at[pl.ds(pl.multiple_of(me * share, share), share), here], out.at[:, there], xlocal.at[g]
        )
        keep.start()
        exchange.append(keep)
    for copy in exchange:
        copy.wait()
    for copy in flights.values():
        copy.wait_send()


def exchange_groups(chunks):
    return [list(range(chunks))[i : i + chunks // 2] for i in (0, chunks // 2)]


def return_partials(acc_all, stat_all, side, peers):
    half = side // 2
    rows = acc_all.shape[2]
    tokens = rows // GROUP
    chunks = 8
    width = GROUP * HD
    groups = len(exchange_groups(chunks))
    message = (2, chunks, half, HD + 8, rows // chunks)
    return pl.pallas_call(
        functools.partial(return_kernel, side),
        out_shape=jax.ShapeDtypeStruct((tokens // peers, peers * width), jnp.bfloat16),
        in_specs=[VMEM] * 2,
        out_specs=HBM,
        scratch_shapes=[
            pltpu.VMEM(message, jnp.bfloat16),
            pltpu.VMEM(message, jnp.bfloat16),
            pltpu.VMEM((tokens, width), jnp.bfloat16),
            pltpu.SemaphoreType.DMA((2, chunks, half)),
            pltpu.SemaphoreType.DMA((2, chunks, half)),
            pltpu.SemaphoreType.DMA((groups, peers)),
            pltpu.SemaphoreType.DMA((groups, peers)),
            pltpu.SemaphoreType.DMA((groups,)),
        ],
        compiler_params=pltpu.CompilerParams(
            collective_id=1, has_side_effects=True, vmem_limit_bytes=16 << 20
        ),
        name="return_partials",
    )(acc_all, stat_all)


def per_device(
    queries,
    new_keys,
    new_values,
    library_keys,
    library_values,
    module_owner,
    module_page,
    module_count,
):
    rows_count = lax.axis_size("rows")
    peers = lax.axis_size("heads")
    side = math.isqrt(rows_count)
    *shards, q_all, table, acc, stat = gather_lines(
        module_owner,
        module_page,
        module_count,
        library_keys,
        library_values,
        queries,
        new_keys,
        new_values,
        side,
    )
    acc_all, stat_all = partials(table, shards, q_all, acc, stat, side)
    return return_partials(acc_all, stat_all, side, peers)


def solution(mesh):
    placed = (
        P("rows", "heads"),
        P("rows", "heads"),
        P("rows", "heads"),
        P("rows", None, "heads"),
        P("rows", None, "heads"),
        P("rows", None),
        P("rows", None),
        P("rows"),
    )
    return jax.shard_map(
        per_device,
        mesh=mesh,
        in_specs=placed,
        out_specs=P(("rows", "heads"), None),
        check_vma=False,
    )
```

```python
import functools
import math

import jax
import jax.numpy as jnp
from jax import lax
from jax.experimental import pallas as pl
from jax.experimental.pallas import tpu as pltpu
from jax.sharding import PartitionSpec as P

HD = 128
QH = 64
KVH = 8
GROUP = QH // KVH
MESH = pl.DeviceIdType.MESH
LOG2E = 1.4426950408889634
FLOOR = -1e30
NEAR_SLOTS = 4
MID_SLOTS = 2
UNROLL = True


def place(side):
    row = lax.axis_index("rows")
    core = lax.rem(lax.axis_index("heads"), 2)
    z, y = row // side, lax.rem(row, side)
    u = (1 - core) * z + core * y
    w = (1 - core) * y + core * z
    return core, u, w


def row_of(core, u, w, side):
    return (1 - core) * (u * side + w) + core * (w * side + u)


def wrap(value, side):
    return lax.rem(value + 4 * side, side)


def accumulate(acc, stat, q_all, req, items, causal=False):
    scale = LOG2E / math.sqrt(HD)
    rows = q_all.shape[2]
    tokens = rows // GROUP
    wide = 2 * tokens
    for c in range(rows // wide):
        cols = slice(c * wide, (c + 1) * wide)
        query = q_all[req, :, cols]
        raws = [jnp.dot(keys, query, preferred_element_type=jnp.float32) for keys, _, _ in items]
        if causal:
            key_at = lax.broadcasted_iota(jnp.int32, raws[0].shape, 0)
            token_at = lax.rem(lax.broadcasted_iota(jnp.int32, raws[0].shape, 1), tokens)
            allowed = key_at <= token_at
            raws = [jnp.where(allowed, raw, FLOOR) for raw in raws]
        old = stat[req, 0:1, cols]
        top = old
        for raw, (_, _, live) in zip(raws, items):
            high = jnp.max(raw, axis=0, keepdims=True) * scale
            top = jnp.maximum(top, high if live is None else jnp.where(live, high, FLOOR))
        shrink = jnp.exp2(old - top)
        total = stat[req, 1:2, cols] * shrink
        mixed = acc[req, :, cols] * shrink
        for raw, (_, values, live) in zip(raws, items):
            base = top if live is None else jnp.where(live, top, -FLOOR)
            weights = jnp.exp2(raw * scale - base)
            if causal:
                weights = jnp.where(allowed, weights, 0.0)
            total = total + jnp.sum(weights, axis=0, keepdims=True)
            mixed = mixed + jnp.dot(values, weights.astype(jnp.bfloat16), preferred_element_type=jnp.float32)
        stat[req, 0:1, cols] = top
        stat[req, 1:2, cols] = total
        acc[req, :, cols] = mixed


def gather_kernel(
    side,
    owner_in, page_in, count, k_in, v_in, q_in, nk_in, nv_in,
    k_near, v_near, k_mid, v_mid, k_far, v_far, q_all, t_all, acc, stat,
    owner, page, table, vraw, qraw, nk, nv, send, recv, local,
):
    core, u, w = place(side)
    half = side // 2
    reach = k_near.shape[0] // 2
    heads_wide = q_all.shape[2] // 2
    shape = t_all.shape[1:]
    lanes = shape[1] // 4
    slots = owner.shape[1]
    pages = k_in.shape[0]
    tokens = qraw.shape[0]
    lib_at = [row_of(core, wrap(u + d, side), w, side) for d in (1, -1)]
    que_at = [row_of(core, u, wrap(w + d, side), side) for d in (1, -1)]

    barrier = pltpu.get_barrier_semaphore()
    for row in lib_at + que_at:
        pl.semaphore_signal(barrier, inc=1, device_id={"rows": row}, device_id_type=MESH)

    def fetch(at, src, dst):
        copy = pltpu.make_async_copy(src, dst, local.at[at])
        copy.start()
        return copy

    lists = [fetch(0, owner_in, owner), fetch(1, page_in, page)]
    fetch_q, fetch_v = fetch(2, q_in, qraw), fetch(3, v_in, vraw)
    own_k = fetch(4, k_in, k_near.at[reach])
    fresh = [fetch(5, nk_in, nk), fetch(6, nv_in, nv)]
    pl.semaphore_wait(barrier, 4)

    def shard(kind, d):
        near, mid, far = ((k_near, k_mid, k_far), (v_near, v_mid, v_far))[kind]
        if abs(d) <= reach:
            return near.at[d + reach]
        return far.at[0] if abs(d) == half else mid.at[(reach - d) // side + 1]

    started = {}
    waited = set()

    def receive(key):
        if key not in waited:
            started[key].wait_recv()
            waited.add(key)

    def start(dirn, step, kind):
        sign = (1, -1)[dirn]
        if step > 0:
            receive((dirn, step - 1, kind))
        if kind < 2:
            src = k_in if step == 0 and kind == 0 else shard(kind, -sign * step)
            dst, row = shard(kind, -sign * (step + 1)), lib_at[dirn]
        else:
            w0 = wrap(w - sign * step, side)
            dst, row = (q_all.at[w0], t_all.at[w0])[kind - 2], que_at[dirn]
            if kind == 2 and step == half - 1:
                dst = dst.at[:, pl.ds(dirn * heads_wide, heads_wide)]
            src = dst
        copy = pltpu.make_async_remote_copy(
            src_ref=src,
            dst_ref=dst,
            send_sem=send.at[dirn, step, kind],
            recv_sem=recv.at[dirn, step, kind],
            device_id={"rows": row},
            device_id_type=MESH,
        )
        copy.start()
        started[dirn, step, kind] = copy

    def both(step, kind):
        for dirn in (0, 1):
            start(dirn, step, kind)

    both(0, 0)
    for copy in lists:
        copy.wait()
    line_at = lax.broadcasted_iota(jnp.int32, shape, 0)
    lane_at = lax.broadcasted_iota(jnp.int32, shape, 1)
    filled = [jnp.full(shape, g * lanes, jnp.int32) for g in range(3)]
    packed = jnp.zeros(shape, jnp.int32)
    for slot in range(slots):
        z, y = owner[0, slot] // side, lax.rem(owner[0, slot], side)
        line = (1 - core) * z + core * y
        cross = (1 - core) * y + core * z
        ahead = wrap(line - u + reach, side)
        listed = jnp.logical_and(line_at == cross, count[0] > slot)
        beyond = ahead - 2 * reach - 1
        groups = (
            (beyond < 0, ahead),
            (jnp.logical_or(beyond == 0, beyond == 2), beyond // 2),
            (beyond == 1, 0),
        )
        for g, (belongs, shard_at) in enumerate(groups):
            hit = jnp.logical_and(listed, belongs)
            spot = shard_at * pages + page[0, slot]
            packed = jnp.where(jnp.logical_and(hit, lane_at == filled[g]), spot, packed)
            filled[g] = filled[g] + jnp.where(hit, 1, 0)
    for g in range(3):
        packed = jnp.where(lane_at == (g + 1) * lanes - 1, filled[g] - g * lanes, packed)
    t_all[w] = packed
    both(0, 3)
    fetch_q.wait()
    for j in range(GROUP):
        q_all[w, :, j * tokens : (j + 1) * tokens] = jnp.transpose(qraw[:, j * HD : (j + 1) * HD])
    both(0, 2)
    fetch_v.wait()
    for j in range(pages):
        v_near[reach, j] = jnp.transpose(vraw[j])
    both(0, 1)
    for step in range(1, half - 1):
        both(step, 3)
    start(0, half - 1, 3)

    @pl.loop(0, side)
    def _(req):
        acc[req] = jnp.zeros(acc.shape[1:], jnp.float32)
        stat[req, 0:1] = jnp.full((1, acc.shape[2]), FLOOR, jnp.float32)
        stat[req, 1:2] = jnp.zeros((1, acc.shape[2]), jnp.float32)

    for copy in fresh:
        copy.wait()
    accumulate(acc, stat, q_all, w, [(nk[...], jnp.transpose(nv[...]), None)], causal=True)
    receive((0, half - 1, 3))
    receive((1, half - 2, 3))
    to_scalars = fetch(7, t_all, table)

    both(1, 0)
    both(1, 2)
    both(1, 1)
    both(2, 2)
    both(2, 0)
    both(3, 2)
    both(2, 1)
    for dirn in (0, 1):
        receive((dirn, half - 1, 2))
    own_k.wait()
    to_scalars.wait()

    def listed(g, most, first, last, keys, values):
        def one(req):
            items = []
            for k in range(most):
                live = k < table[req, w, (g + 1) * lanes - 1]
                spot = table[req, w, g * lanes + k]
                shard_at, page_at = spot // pages, lax.rem(spot, pages)
                items.append((keys[shard_at, page_at], values[shard_at, page_at], live))
            accumulate(acc, stat, q_all, req, items)

        if UNROLL:
            for req in range(first, last):
                one(req)
        else:
            pl.loop(first, last)(one)

    listed(0, NEAR_SLOTS, 0, half, k_near, v_near)
    start(0, half - 1, 0)
    start(1, half - 1, 1)
    listed(0, NEAR_SLOTS, half, side, k_near, v_near)
    for dirn in (0, 1):
        for kind in (0, 1):
            receive((dirn, half - 2, kind))
    listed(1, MID_SLOTS, 0, side, k_mid, v_mid)
    for key in started:
        receive(key)
    for copy in started.values():
        copy.wait_send()


HBM = pl.BlockSpec(memory_space=pltpu.HBM)
SMEM = pl.BlockSpec(memory_space=pltpu.SMEM)
VMEM = pl.BlockSpec(memory_space=pltpu.VMEM)


def in_hbm(a):
    return pltpu.with_memory_space_constraint(a, pltpu.HBM)


def gather_lines(owner, page, count, k, v, q, nk, nv, side):
    half = side // 2
    tokens = q.shape[0]
    near = 2 * (half - 2) + 1
    return pl.pallas_call(
        functools.partial(gather_kernel, side),
        out_shape=[
            *[pltpu.VMEM((n,) + a.shape, a.dtype) for n in (near, 2, 1) for a in (k, v)],
            pltpu.VMEM((side, HD, GROUP * tokens), q.dtype),
            pltpu.VMEM((side, side, 128), jnp.int32),
            pltpu.VMEM((side, HD, GROUP * tokens), jnp.float32),
            pltpu.VMEM((side, 2, GROUP * tokens), jnp.float32),
        ],
        in_specs=[HBM, HBM, SMEM] + [HBM] * 5,
        out_specs=[VMEM] * 10,
        scratch_shapes=[
            pltpu.SMEM(owner.shape, owner.dtype),
            pltpu.SMEM(page.shape, page.dtype),
            pltpu.SMEM((side, side, 128), jnp.int32),
            pltpu.VMEM(v.shape, v.dtype),
            pltpu.VMEM(q.shape, q.dtype),
            pltpu.VMEM(nk.shape, nk.dtype),
            pltpu.VMEM(nv.shape, nv.dtype),
            pltpu.SemaphoreType.DMA((2, half, 4)),
            pltpu.SemaphoreType.DMA((2, half, 4)),
            pltpu.SemaphoreType.DMA((8,)),
        ],
        compiler_params=pltpu.CompilerParams(
            collective_id=0, has_side_effects=True, vmem_limit_bytes=16 << 20
        ),
        name="gather_lines",
    )(in_hbm(owner), in_hbm(page), count, *[in_hbm(a) for a in (k, v, q, nk, nv)])


def partial_kernel(side, table, *refs):
    shards, (q_all, _, _, acc, stat) = refs[:-5], refs[-5:]
    _, _, w = place(side)
    pages = shards[0].shape[1]
    lanes = table.shape[2] // 4

    @pl.loop(0, side)
    def _(req):
        for g, done in enumerate((NEAR_SLOTS, MID_SLOTS, 0)):
            keys, values = shards[2 * g], shards[2 * g + 1]

            @pl.loop(done, jnp.maximum(table[req, w, (g + 1) * lanes - 1], done))
            def _(k):
                spot = table[req, w, g * lanes + k]
                shard_at, page_at = spot // pages, lax.rem(spot, pages)
                accumulate(acc, stat, q_all, req, [(keys[shard_at, page_at], values[shard_at, page_at], None)])


def partials(table, shards, q_all, acc, stat, side):
    first = 2 + len(shards)
    return pl.pallas_call(
        functools.partial(partial_kernel, side),
        out_shape=[pltpu.VMEM(acc.shape, acc.dtype), pltpu.VMEM(stat.shape, stat.dtype)],
        in_specs=[SMEM] + [VMEM] * (first + 1),
        out_specs=[VMEM, VMEM],
        input_output_aliases={first: 0, first + 1: 1},
        compiler_params=pltpu.CompilerParams(vmem_limit_bytes=16 << 20),
        name="partials",
    )(table, *shards, q_all, acc, stat)


def return_kernel(side, accs, stats, out, outgoing, incoming, result, send, recv, xsend, xrecv, xlocal):
    core, u, w = place(side)
    me = lax.axis_index("heads")
    peers = lax.axis_size("heads")
    half = side // 2
    chunks = outgoing.shape[1]
    part = outgoing.shape[4]
    extra = outgoing.shape[3] - HD
    tokens, width = result.shape
    share = tokens // peers
    near = [row_of(core, u, wrap(w + d, side), side) for d in (1, -1)]

    barrier = pltpu.get_barrier_semaphore()
    for row in near:
        pl.semaphore_signal(barrier, inc=1, device_id={"rows": row}, device_id_type=MESH)
    for hop in range(1, peers):
        pl.semaphore_signal(
            barrier, inc=1, device_id={"heads": lax.rem(me + hop, peers)}, device_id_type=MESH
        )

    def far(dirn, c):
        return half if c % 2 == dirn else half - 1

    def mine(d, c):
        target, cols = wrap(w + d, side), slice(c * part, (c + 1) * part)
        return accs[target, :, cols], stats[target, 0:1, cols], stats[target, 1:2, cols]

    def split(value):
        pieces = []
        for _ in range(3):
            pieces.append(value.astype(jnp.bfloat16).astype(jnp.float32))
            value = value - pieces[-1]
        return pieces

    row_at = lax.broadcasted_iota(jnp.int32, (extra, part), 0)

    def pack(ref, item):
        acc, top, total = item
        ref[0:HD] = acc.astype(jnp.bfloat16)
        tail = jnp.zeros((extra, part), jnp.float32)
        for i, piece in enumerate(split(top) + split(total)):
            tail = jnp.where(row_at == i, piece, tail)
        ref[HD : HD + extra] = tail.astype(jnp.bfloat16)

    def unpack(ref):
        tail = ref[HD : HD + extra].astype(jnp.float32)
        top = tail[0:1] + tail[1:2] + tail[2:3]
        total = tail[3:4] + tail[4:5] + tail[5:6]
        return ref[0:HD].astype(jnp.float32), top, total

    def merge(one, two):
        top = jnp.maximum(one[1], two[1])
        fa, fb = jnp.exp2(one[1] - top), jnp.exp2(two[1] - top)
        return one[0] * fa + two[0] * fb, top, one[2] * fa + two[2] * fb

    flights = {}

    def launch(dirn, c, k):
        copy = pltpu.make_async_remote_copy(
            src_ref=outgoing.at[dirn, c, k],
            dst_ref=incoming.at[dirn, c, k],
            send_sem=send.at[dirn, c, k],
            recv_sem=recv.at[dirn, c, k],
            device_id={"rows": near[dirn]},
            device_id_type=MESH,
        )
        copy.start()
        flights[dirn, c, k] = copy

    def arrived(dirn, c, k):
        flights[dirn, c, k].wait_recv()
        return unpack(incoming.at[dirn, c, k])

    starts = sorted(((c, dirn) for c in range(chunks) for dirn in (0, 1)), key=lambda at: -far(at[1], at[0]))
    for c, dirn in starts:
        pack(outgoing.at[dirn, c, 0], mine((1, -1)[dirn] * far(dirn, c), c))
    pl.semaphore_wait(barrier, 1 + peers)
    for c, dirn in starts:
        launch(dirn, c, 0)
    for k in range(1, half):
        for c, dirn in starts:
            reach = far(dirn, c) - k
            if reach < 1:
                continue
            item = mine((1, -1)[dirn] * reach, c)
            pack(outgoing.at[dirn, c, k], merge(item, arrived(dirn, c, k - 1)))
            launch(dirn, c, k)

    exchange = []
    groups = exchange_groups(chunks)
    for g, group in enumerate(groups):
        for c in group:
            item = mine(0, c)
            for dirn in sorted((0, 1), key=lambda dirn: far(dirn, c)):
                item = merge(item, arrived(dirn, c, far(dirn, c) - 1))
            final = item[0] / item[2]
            for j in range(part // tokens):
                at = c * part // tokens + j
                block = jnp.transpose(final[:, j * tokens : (j + 1) * tokens].astype(result.dtype))
                result[:, at * HD : (at + 1) * HD] = block
        first, size = group[0] * part, len(group) * part
        here = slice(first, first + size)
        there = pl.ds(pl.multiple_of(me * width + first, size), size)
        for hop in sorted(range(1, peers), key=lambda hop: abs(hop - peers // 2)):
            peer = lax.rem(me + hop, peers)
            copy = pltpu.make_async_remote_copy(
                src_ref=result.at[pl.ds(pl.multiple_of(peer * share, share), share), here],
                dst_ref=out.at[:, there],
                send_sem=xsend.at[g, hop],
                recv_sem=xrecv.at[g, hop],
                device_id={"heads": peer},
                device_id_type=MESH,
            )
            copy.start()
            exchange.append(copy)
        keep = pltpu.make_async_copy(
            result.at[pl.ds(pl.multiple_of(me * share, share), share), here], out.at[:, there], xlocal.at[g]
        )
        keep.start()
        exchange.append(keep)
    for copy in exchange:
        copy.wait()
    for copy in flights.values():
        copy.wait_send()


def exchange_groups(chunks):
    return [list(range(chunks))[i : i + chunks // 2] for i in (0, chunks // 2)]


def return_partials(acc_all, stat_all, side, peers):
    half = side // 2
    rows = acc_all.shape[2]
    tokens = rows // GROUP
    chunks = 8
    width = GROUP * HD
    groups = len(exchange_groups(chunks))
    message = (2, chunks, half, HD + 8, rows // chunks)
    return pl.pallas_call(
        functools.partial(return_kernel, side),
        out_shape=jax.ShapeDtypeStruct((tokens // peers, peers * width), jnp.bfloat16),
        in_specs=[VMEM] * 2,
        out_specs=HBM,
        scratch_shapes=[
            pltpu.VMEM(message, jnp.bfloat16),
            pltpu.VMEM(message, jnp.bfloat16),
            pltpu.VMEM((tokens, width), jnp.bfloat16),
            pltpu.SemaphoreType.DMA((2, chunks, half)),
            pltpu.SemaphoreType.DMA((2, chunks, half)),
            pltpu.SemaphoreType.DMA((groups, peers)),
            pltpu.SemaphoreType.DMA((groups, peers)),
            pltpu.SemaphoreType.DMA((groups,)),
        ],
        compiler_params=pltpu.CompilerParams(
            collective_id=1, has_side_effects=True, vmem_limit_bytes=16 << 20
        ),
        name="return_partials",
    )(acc_all, stat_all)


def per_device(
    queries,
    new_keys,
    new_values,
    library_keys,
    library_values,
    module_owner,
    module_page,
    module_count,
):
    rows_count = lax.axis_size("rows")
    peers = lax.axis_size("heads")
    side = math.isqrt(rows_count)
    *shards, q_all, table, acc, stat = gather_lines(
        module_owner,
        module_page,
        module_count,
        library_keys,
        library_values,
        queries,
        new_keys,
        new_values,
        side,
    )
    acc_all, stat_all = partials(table, shards, q_all, acc, stat, side)
    return return_partials(acc_all, stat_all, side, peers)


def solution(mesh):
    placed = (
        P("rows", "heads"),
        P("rows", "heads"),
        P("rows", "heads"),
        P("rows", None, "heads"),
        P("rows", None, "heads"),
        P("rows", None),
        P("rows", None),
        P("rows"),
    )
    return jax.shard_map(
        per_device,
        mesh=mesh,
        in_specs=placed,
        out_specs=P(("rows", "heads"), None),
        check_vma=False,
    )
```
